128 devices in a mesh: expert: 8 (over x, core), hidden: 16 (over z, y).
Axes of the slice: x: 4, y: 4, z: 4, core: 2. Of those that a mesh axis runs over, the one named last changes fastest.
Arguments:
- hidden_in: bfloat16 [2048, 6144], P(('expert', 'hidden')), may hold values from -6 to 6
- norm_gain: float32 [6144], replicated, may hold values from 0.25 to 1.75
- router_weight: bfloat16 [6144, 8], replicated, may hold values from -0.078125 to 0.078125
- expert_ids: int32 [2048, 2], P(('expert', 'hidden')), may hold values from 0 to 7, all different within a row; in each aligned block of 16 rows (0 to 15, 16 to 31, ...) at most 6 rows name the same one
- gate_proj: bfloat16 [8, 6144, 8192], P('expert', None, 'hidden'), may hold values from -0.078125 to 0.078125
- up_proj: bfloat16 [8, 6144, 8192], P('expert', None, 'hidden'), may hold values from -0.078125 to 0.078125
- down_proj: bfloat16 [8, 8192, 6144], P('expert', 'hidden'), may hold values from -0.0625 to 0.0625
Outputs:
- layer_out: bfloat16 [2048, 6144], P(('expert', 'hidden'))
The draws below stay inside these ranges and needn't reach their ends.
Inputs may be any that keep to these rules, and one draw needn't show every extreme that they name: `expert_ids`: the two experts of a token differ. Within the rows of one device (aligned blocks of 16 tokens) no expert is named by more than 6 rows, a bound that some block reaches.
All inputs are finite; a program needn't handle non-finite values.
Results may differ from the reference program's by a relative error of at most 0.0085.
Values may be sent and summed in bfloat16 or wider, within the bound.
No kernel may reach another device: no remote copies, remote signals or barrier semaphores. Data moves between devices by JAX's collectives and lax.ppermute only.
A program may use at most 128 MiB of HBM per device.

```python
import math
import jax
import jax.numpy as jnp
import numpy as np
from jax import lax

D = 6144
FF = 8192
TOP = 2
TOK_DEV = 16
EXPERTS = 8
CAP = 6
TOKENS = 2048
N_EXPERT = 8
N_HIDDEN = 16


def block_scale(rng, extent, cuts, least, high):
    level, own = 1.0, jax.random.fold_in(rng, 6)
    for dim, shards_of in cuts:
        steps = jnp.exp(jax.random.uniform(jax.random.fold_in(own, dim), (shards_of,), jnp.float32, least / len(cuts), high / len(cuts)))
        level = level * jnp.repeat(steps, extent[dim] // shards_of).reshape([-1 if axis == dim else 1 for axis in range(len(extent))])
    return level


def routed_block(stream_key, own, number, rows, number_of, top, most, lean):
    sequence = jax.random.permutation(stream_key, number_of)
    crowded, common = load_shares(number_of, rows * top, most, lean, True), load_shares(number_of, rows * top, most, lean, False)
    places = jnp.arange(number_of)

    def named(tallies, rotation):
        used = int((tallies > 0).sum())
        fixed = max(1, used // 4)
        moved = fixed + (places - fixed + rotation * (used - fixed)) % max(1, number_of - fixed)
        return jnp.zeros((number_of,), jnp.int32).at[sequence[jnp.where(places < fixed, places, moved)]].set(jnp.asarray(tallies, jnp.int32))

    tallies = jnp.where(number % 4 == 0, named(crowded, number // 4), named(common, number - number // 4 - 1))
    mixed = jax.random.permutation(jax.random.fold_in(own, 3), number_of)
    source_of, sink = mixed[0:number_of // 2 * 2:2], mixed[1:number_of // 2 * 2:2]
    margin = jnp.minimum(tallies[source_of] - 1, most - tallies[sink]) // 2
    margin = jnp.where((source_of == sequence[0]) | (sink == sequence[0]) | (tallies[sink] == 0), 0, jnp.maximum(margin, 0))
    moved = jax.random.randint(jax.random.fold_in(own, 4), (number_of // 2,), 0, 1 << 20) % (margin + 1)
    tallies = tallies.at[source_of].add(-moved).at[sink].add(moved)
    members = jnp.searchsorted(jnp.cumsum(tallies), jnp.arange(rows * top), side="right").astype(jnp.int32)
    table = members.reshape(top, rows).T
    table = table[jax.random.permutation(jax.random.fold_in(own, 1), rows)]
    rotation = jax.random.randint(jax.random.fold_in(own, 2), (rows, 1), 0, top)
    return jnp.take_along_axis(table, (jnp.arange(top)[None, :] + rotation) % top, axis=1)


def load_shares(amount, total, limit, lean, full):
    loads = [(1 << 20) // math.isqrt(grade ** lean) + 1 for grade in range(1, amount + 1)]
    largest = limit if full else min(limit, max(-(-total // amount), total * loads[0] // sum(loads)))
    least = 1 if total - largest >= amount - 1 else 0
    given, surplus = [largest] + [least] * (amount - 1), total - largest - least * (amount - 1)
    while surplus > 0:
        free = [i for i in range(1, amount) if given[i] < largest] or [i for i in range(1, amount) if given[i] < limit]
        whole, remaining = sum([loads[i] for i in free]), surplus
        for i in free:
            more = min(limit - given[i], max(1, remaining * loads[i] // whole), surplus)
            given[i] = given[i] + more
            surplus = surplus - more
    return np.array(given)


def noise(rng, shape, deviation, limit, pieces=(), held_as=jnp.bfloat16):
    result = deviation * jax.random.normal(rng, shape, jnp.float32)
    if pieces:
        result = result * block_scale(rng, shape, pieces, -0.22, 0.18)
    return jnp.clip(result, -limit, limit).astype(held_as)


def setup_inputs(seed: int = 0) -> dict:
    streams_of = jax.random.split(jax.random.key(seed), 8)
    hidden_in = noise(streams_of[0], (TOKENS, D), 1.0, 6.0, ((0, 128),))
    norm_gain = jnp.clip(1.0 + 0.15 * jax.random.normal(streams_of[1], (D,), jnp.float32), 0.25, 1.75)
    router_weight = noise(streams_of[2], (D, EXPERTS), D ** -0.5, 0.078125)
    expert_ids_keys = jax.random.split(jax.random.fold_in(streams_of[3], 1), TOKENS // TOK_DEV)
    expert_ids_turns = jax.random.permutation(jax.random.fold_in(streams_of[3], 3), TOKENS // TOK_DEV)
    expert_ids = jax.vmap(lambda own, number: routed_block(jax.random.fold_in(streams_of[3], 2), own, number, TOK_DEV, EXPERTS, TOP, CAP, 2))(expert_ids_keys, expert_ids_turns).reshape((TOKENS, TOP))
    gate_proj = noise(streams_of[4], (EXPERTS, D, FF), D ** -0.5, 0.078125, ((0, 8), (2, 16)))
    up_proj = noise(streams_of[5], (EXPERTS, D, FF), D ** -0.5, 0.078125, ((0, 8), (2, 16)))
    down_proj = noise(streams_of[6], (EXPERTS, FF, D), FF ** -0.5, 0.0625, ((0, 8), (1, 16)))
    return dict(hidden_in=hidden_in, norm_gain=norm_gain, router_weight=router_weight, expert_ids=expert_ids, gate_proj=gate_proj, up_proj=up_proj, down_proj=down_proj)


def normalize(hidden_in, norm_gain):
    values = hidden_in.astype(jnp.float32)
    factor = lax.rsqrt(lax.optimization_barrier(jnp.mean(values * values, axis=-1, keepdims=True)) + 1e-05)
    return (values * factor * norm_gain).astype(jnp.bfloat16)

def gate_weights(normed, router_weight, expert_ids, experts):
    logits = jnp.dot(normed, router_weight, preferred_element_type=jnp.float32)
    picks = expert_ids[:, :, None] == jnp.arange(experts, dtype=jnp.int32)[None, None, :]
    chosen = lax.optimization_barrier(jnp.sum(jnp.where(picks, logits[:, None, :], 0.0), axis=-1))
    first = jax.nn.sigmoid(chosen[:, 0] - chosen[:, 1])
    return jnp.stack([first, 1.0 - first], axis=1)

def route_slots(block_ids, experts, capacity):
    flat_ids = block_ids.reshape(-1)
    onehot = (flat_ids[:, None] == jnp.arange(experts, dtype=jnp.int32)[None, :]).astype(jnp.int32)
    before = jnp.cumsum(onehot, axis=0) - onehot
    rank_in = lax.optimization_barrier(jnp.sum(before * onehot, axis=1))
    slot_place = (flat_ids * capacity + rank_in).astype(jnp.int32)
    owners = (jnp.arange(flat_ids.shape[0], dtype=jnp.int32) // block_ids.shape[1]).astype(jnp.int32)
    slot_token = jnp.zeros((experts * capacity,), jnp.int32).at[slot_place].set(owners)
    filled = jnp.zeros((experts * capacity,), jnp.bfloat16).at[slot_place].set(1.0)
    return (slot_place, slot_token, filled)

def expert_rows(rows, gate_w, up_w, down_w):
    gate = jnp.dot(rows, gate_w, preferred_element_type=jnp.float32)
    upper = jnp.dot(rows, up_w, preferred_element_type=jnp.float32)
    inner = (jax.nn.silu(gate) * upper).astype(jnp.bfloat16)
    block_width = FF // N_HIDDEN

    def add_block(total, index):
        start = index * block_width
        piece_h = lax.dynamic_slice_in_dim(inner, start, block_width, 1)
        piece_w = lax.dynamic_slice_in_dim(down_w, start, block_width, 0)
        term = jnp.dot(piece_h, piece_w, preferred_element_type=jnp.float32).astype(jnp.bfloat16)
        term = lax.optimization_barrier(term)
        return (total + term.astype(jnp.float32), None)
    total, _ = lax.scan(add_block, jnp.zeros((rows.shape[0], D), jnp.float32), jnp.arange(N_HIDDEN, dtype=jnp.int32))
    return total.astype(jnp.bfloat16)

def fill_block(normed_block, slot_token, filled):
    return jnp.take(normed_block, slot_token, axis=0) * filled[:, None]

def pick_block(returned_block, slot_place):
    return jnp.take(returned_block, slot_place, axis=0)

def route_block(block_ids):
    return route_slots(block_ids, EXPERTS, CAP)

def run_expert(packed):
    return expert_rows(packed[0], packed[1], packed[2], packed[3])

def reference(hidden_in, norm_gain, router_weight, expert_ids, gate_proj, up_proj, down_proj):
    blocks = N_EXPERT * N_HIDDEN
    normed = normalize(hidden_in, norm_gain)
    gates = gate_weights(normed, router_weight, expert_ids, EXPERTS)
    slot_place, slot_token, filled = jax.vmap(route_block)(expert_ids.reshape(blocks, TOK_DEV, TOP))
    buffers = jax.vmap(fill_block)(normed.reshape(blocks, TOK_DEV, D), slot_token, filled)
    per_expert = buffers.reshape(blocks, EXPERTS, CAP, D).transpose(1, 0, 2, 3).reshape(EXPERTS, blocks * CAP, D)
    outputs = lax.map(run_expert, (per_expert, gate_proj, up_proj, down_proj))
    returned = outputs.reshape(EXPERTS, blocks, CAP, D).transpose(1, 0, 2, 3).reshape(blocks, EXPERTS * CAP, D)
    picked = jax.vmap(pick_block)(returned, slot_place).reshape(TOKENS, TOP, D).astype(jnp.float32)
    mixture = lax.optimization_barrier(jnp.sum(gates[:, :, None] * picked, axis=1))
    return (hidden_in.astype(jnp.float32) + mixture).astype(jnp.bfloat16)
```

```python
import jax
import jax.numpy as jnp
from jax import lax
from jax.sharding import PartitionSpec as P


ROUNDS = ((4, 12, 1, 3), (12, 4, 3, 1), (1, 3, 4, 12), (3, 1, 12, 4))
ORDER = ((0, 1, 2, 3), (1, 0, 3, 2), (2, 3, 0, 1), (3, 2, 1, 0))


def normalize(hidden_in, norm_gain):
    values = hidden_in.astype(jnp.float32)
    factor = lax.rsqrt(jnp.mean(values * values, axis=-1, keepdims=True) + 1e-05)
    return (values * factor * norm_gain).astype(jnp.bfloat16)


def gate_weights(normed, router_weight, expert_ids, experts):
    logits = jnp.dot(normed, router_weight, preferred_element_type=jnp.float32)
    picks = expert_ids[:, :, None] == jnp.arange(experts, dtype=jnp.int32)[None, None, :]
    chosen = jnp.sum(jnp.where(picks, logits[:, None, :], 0.0), axis=-1)
    first = jax.nn.sigmoid(chosen[:, 0] - chosen[:, 1])
    return jnp.stack([first, 1.0 - first], axis=1)


def route_slots(block_ids, experts, capacity):
    flat_ids = block_ids.reshape(-1)
    onehot = (flat_ids[:, None] == jnp.arange(experts, dtype=jnp.int32)[None, :]).astype(jnp.int32)
    before = jnp.cumsum(onehot, axis=0) - onehot
    rank_in = jnp.sum(before * onehot, axis=1)
    slot_place = flat_ids * capacity + rank_in
    owners = jnp.arange(flat_ids.shape[0], dtype=jnp.int32) // block_ids.shape[1]
    slot_token = jnp.zeros((experts * capacity,), jnp.int32).at[slot_place].set(owners)
    filled = jnp.zeros((experts * capacity,), jnp.bfloat16).at[slot_place].set(1.0)
    return (slot_place, slot_token, filled)


def swap(value, mask, count):
    return lax.ppermute(value, "hidden", [(i, i ^ mask) for i in range(count)])


def reorder(value, group, rows):
    shaped = value.reshape(2, 2, 2, 2, rows, value.shape[1])
    return shaped.transpose(*ORDER[group], 4, 5)


def per_device(hidden_in, norm_gain, router_weight, expert_ids, gate_proj, up_proj, down_proj):
    experts = lax.axis_size("expert")
    hidden_count = lax.axis_size("hidden")
    tok_rows = hidden_in.shape[0]
    width = hidden_in.shape[1]
    top_count = expert_ids.shape[1]
    capacity = 3 * tok_rows * top_count // (2 * experts)
    rows = experts * capacity
    groups = len(ROUNDS)
    part = width // groups
    normed = normalize(hidden_in, norm_gain)
    gates = gate_weights(normed, router_weight, expert_ids, experts)
    slot_place, slot_token, filled = route_slots(expert_ids, experts, capacity)
    outgoing = (jnp.take(normed, slot_token, axis=0) * filled[:, None]).reshape(
        experts, capacity, width
    )
    gate_local = gate_proj[0]
    up_local = up_proj[0]
    down_local = down_proj[0]
    arrived = lax.all_to_all(outgoing, "expert", split_axis=0, concat_axis=0, tiled=True)
    arrived = arrived.reshape(rows, width)
    held = [arrived[:, g * part : (g + 1) * part] for g in range(groups)]
    for step in range(3):
        other = [swap(held[g], ROUNDS[g][step], hidden_count) for g in range(groups)]
        held = [jnp.concatenate([a, b], axis=0) for a, b in zip(held, other)]
    late = [swap(held[g], ROUNDS[g][3], hidden_count) for g in range(groups)]

    def project(weight):
        total = 0.0
        for g in range(groups):
            block = weight[g * part : (g + 1) * part]
            near = jnp.dot(held[g], block, preferred_element_type=jnp.float32)
            far = jnp.dot(late[g], block, preferred_element_type=jnp.float32)
            total = total + reorder(jnp.concatenate([near, far], axis=0), g, rows)
        return total

    inner = (jax.nn.silu(project(gate_local)) * project(up_local)).astype(jnp.bfloat16)
    keep, send = [], []
    for g in range(groups):
        ordered = inner.transpose(*ORDER[g], 4, 5).reshape(2, 8 * rows, inner.shape[5])
        block = down_local[:, g * part : (g + 1) * part]
        send.append(jnp.dot(ordered[1], block, preferred_element_type=jnp.float32).astype(jnp.bfloat16))
        keep.append(jnp.dot(ordered[0], block, preferred_element_type=jnp.float32).astype(jnp.bfloat16))
    for step in (3, 2, 1, 0):
        other = [swap(send[g], ROUNDS[g][step], hidden_count) for g in range(groups)]
        total = [
            (a.astype(jnp.float32) + b.astype(jnp.float32)).astype(jnp.bfloat16)
            for a, b in zip(keep, other)
        ]
        half = total[0].shape[0] // 2
        keep = [t[:half] for t in total] if step else total
        send = [t[half:] for t in total]
    answers = jnp.concatenate(keep, axis=1).reshape(experts, capacity, width)
    returned = lax.all_to_all(answers, "expert", split_axis=0, concat_axis=0, tiled=True).reshape(
        rows, width
    )
    picked = (
        jnp.take(returned, slot_place, axis=0)
        .reshape(tok_rows, top_count, width)
        .astype(jnp.float32)
    )
    mixture = jnp.sum(gates[:, :, None] * picked, axis=1)
    return (hidden_in.astype(jnp.float32) + mixture).astype(jnp.bfloat16)


def solution(mesh):
    placed = (
        P(("expert", "hidden"), None),
        P(),
        P(),
        P(("expert", "hidden"), None),
        P("expert", None, "hidden"),
        P("expert", None, "hidden"),
        P("expert", "hidden", None),
    )
    return jax.shard_map(
        per_device,
        mesh=mesh,
        in_specs=placed,
        out_specs=P(("expert", "hidden"), None),
        check_vma=False,
    )
```

```python
import jax
import jax.numpy as jnp
from jax import lax
from jax.experimental import pallas as pl
from jax.experimental.pallas import tpu as pltpu
from jax.sharding import PartitionSpec as P


RING = 4


PAD = 8
CHUNK = 512


def slots(ids_ref):
    first, second = ids_ref[0:1, :], ids_ref[1:2, :]
    tokens = first.shape[1]
    down = lax.broadcasted_iota(jnp.int32, (tokens, tokens), 0)
    across = lax.broadcasted_iota(jnp.int32, (tokens, tokens), 1)

    def column(row):
        return jnp.sum(jnp.where(down == across, row, 0), axis=1, keepdims=True)

    first_col, second_col = column(first), column(second)
    found = []
    for ids in (first, second):
        same = (first_col == ids).astype(jnp.int32) + (second_col == ids).astype(jnp.int32)
        rank = jnp.sum(jnp.where(down < across, same, 0), axis=0, keepdims=True)
        found.append((ids, rank))
    same = (first == second).astype(jnp.int32)
    return [found[0][0] * PAD + found[0][1], found[1][0] * PAD + found[1][1] + same]


def route_kernel(hidden_ref, gain_ref, ids_ref, out_ref, normed_ref):
    experts, capacity, width = out_ref.shape
    tokens = hidden_ref.shape[0]
    values = hidden_ref[...].astype(jnp.float32)
    factor = lax.rsqrt(jnp.sum(values * values, axis=1, keepdims=True) / width + 1e-05)
    normed_ref[...] = (values * factor * gain_ref[...]).astype(jnp.bfloat16)
    first, second = slots(ids_ref)
    place = lax.broadcasted_iota(jnp.int32, (experts * PAD, tokens), 0)
    pick = jnp.where((place == first) | (place == second), 1.0, 0.0).astype(jnp.bfloat16)

    @pl.loop(0, width // CHUNK)
    def _(step):
        columns = pl.ds(pl.multiple_of(step * CHUNK, CHUNK), CHUNK)
        rows = jnp.dot(pick, normed_ref[:, columns], preferred_element_type=jnp.float32)
        for e in range(experts):
            out_ref[e, :, columns] = rows[e * PAD : e * PAD + capacity].astype(jnp.bfloat16)


def gate_kernel(normed_ref, router_ref, ids_ref, out_ref):
    logits = lax.dot_general(
        router_ref[...], normed_ref[...], (((1,), (1,)), ((), ())), preferred_element_type=jnp.float32
    )
    expert = lax.broadcasted_iota(jnp.int32, logits.shape, 0)
    chosen = [
        jnp.sum(jnp.where(expert == ids_ref[k : k + 1, :], logits, 0.0), axis=0, keepdims=True)
        for k in range(2)
    ]
    gate = 1.0 / (1.0 + jnp.exp(chosen[1] - chosen[0]))
    first, second = slots(ids_ref)
    place = lax.broadcasted_iota(jnp.int32, out_ref.shape, 0)
    out_ref[...] = jnp.where(place == first, gate, 0.0) + jnp.where(place == second, 1.0 - gate, 0.0)


def mix_kernel(hidden_ref, weight_ref, rows_ref, out_ref, held_ref):
    experts, capacity, width = rows_ref.shape
    held_ref[...] = jnp.zeros_like(held_ref)
    weight = weight_ref[...]

    @pl.loop(0, width // CHUNK)
    def _(step):
        columns = pl.ds(pl.multiple_of(step * CHUNK, CHUNK), CHUNK)
        for e in range(experts):
            held_ref[e * PAD : e * PAD + capacity, :] = rows_ref[e, :, columns].astype(jnp.float32)
        mixed = lax.dot_general(
            weight,
            held_ref[...],
            (((0,), (0,)), ((), ())),
            precision=lax.Precision.HIGHEST,
            preferred_element_type=jnp.float32,
        )
        out_ref[:, columns] = (hidden_ref[:, columns].astype(jnp.float32) + mixed).astype(jnp.bfloat16)


def shift(value, axis, step):
    def target(i):
        z, y = divmod(i, RING)
        return ((z + step) % RING) * RING + y if axis == "z" else z * RING + (y + step) % RING

    return lax.ppermute(value, "hidden", [(i, target(i)) for i in range(RING * RING)])


def gather_ring(own, first, second):
    half = own.shape[1] // 2
    below, above = shift(own, first, 1), shift(own, first, -1)
    across = [shift(below[:, :half], first, 1), shift(above[:, half:], first, -1)]
    mine = jnp.concatenate([own, below, above, jnp.concatenate(across, axis=1)], axis=0)
    mine = lax.optimization_barrier(mine)
    rows = mine.shape[0] // 2
    below, above = shift(mine, second, 1), shift(mine, second, -1)
    far = [shift(below[:rows], second, 1), shift(above[rows:], second, -1)]
    return [mine], [below, above], far


def add(*terms):
    total = terms[0].astype(jnp.float32)
    for term in terms[1:]:
        total = total + term.astype(jnp.float32)
    return total.astype(jnp.bfloat16)


def low_add(value, low, half):
    return jnp.concatenate([add(value[:, :half], low), value[:, half:]], axis=1)


def high_add(value, high, half):
    return jnp.concatenate([value[:, :half], add(value[:, half:], high)], axis=1)


def reduce_ring(inner, down, first, second, rows):
    half = down.shape[1] // 2

    def product(blocks, weight):
        value = jnp.concatenate(blocks, axis=0)
        value = jnp.dot(value, weight, preferred_element_type=jnp.float32)
        return lax.optimization_barrier(value.astype(jnp.bfloat16))

    low, high = down[:, :half], down[:, half:]
    early = [inner[b][3] for b in range(3)]
    late = [inner[3][3]]
    lows = [shift(product(t, low), first, 1) for t in (early, late)]
    highs = [shift(product(t, high), first, -1) for t in (early, late)]
    above = product([inner[b][2] for b in range(4)], down)
    below = product([inner[b][1] for b in range(4)], down)
    own = product([inner[b][0] for b in range(4)], down)
    above = shift(low_add(above, jnp.concatenate(lows, axis=0), half), first, 1)
    below = shift(high_add(below, jnp.concatenate(highs, axis=0), half), first, -1)
    own = add(own, above, below)
    across = own[3 * rows :]
    low = shift(across[:, :half], second, 1)
    high = shift(across[:, half:], second, -1)
    above = shift(low_add(own[2 * rows : 3 * rows], low, half), second, 1)
    below = shift(high_add(own[rows : 2 * rows], high, half), second, -1)
    return add(own[:rows], above, below)


def per_device(hidden_in, norm_gain, router_weight, expert_ids, gate_proj, up_proj, down_proj):
    experts = lax.axis_size("expert")
    tok_rows = hidden_in.shape[0]
    width = hidden_in.shape[1]
    top_count = expert_ids.shape[1]
    capacity = 3 * tok_rows * top_count // (2 * experts)
    rows = experts * capacity
    ids = expert_ids.T
    outgoing, normed = pl.pallas_call(
        route_kernel,
        out_shape=(
            jax.ShapeDtypeStruct((experts, capacity, width), jnp.bfloat16),
            jax.ShapeDtypeStruct((tok_rows, width), jnp.bfloat16),
        ),
        name="route",
    )(hidden_in, norm_gain.reshape(1, width), ids)
    weights = pl.pallas_call(
        gate_kernel,
        out_shape=jax.ShapeDtypeStruct((experts * PAD, tok_rows), jnp.float32),
        name="gates",
    )(normed, router_weight.T, ids)
    gate_local = gate_proj[0]
    up_local = up_proj[0]
    down_local = down_proj[0]
    arrived = lax.all_to_all(outgoing, "expert", split_axis=0, concat_axis=0, tiled=True)
    arrived = arrived.reshape(rows, width)
    part = rows // 2
    orders = (("z", "y"), ("y", "z"))
    gathered = [gather_ring(arrived[i * part : (i + 1) * part], *orders[i]) for i in range(2)]
    inner = [[], []]
    for stage in range(3):
        value = jnp.concatenate(gathered[0][stage] + gathered[1][stage], axis=0)
        gate = jnp.dot(value, gate_local, preferred_element_type=jnp.float32)
        upper = jnp.dot(value, up_local, preferred_element_type=jnp.float32)
        act = (jax.nn.silu(gate) * upper).astype(jnp.bfloat16)
        act = act.reshape(2, -1, RING, part, act.shape[1])
        for i in range(2):
            inner[i] += [[act[i, b, a] for a in range(RING)] for b in range(act.shape[1])]
    answers = [reduce_ring(inner[i], down_local, *orders[i], part) for i in range(2)]
    answers = jnp.concatenate(answers, axis=0).reshape(experts, capacity, width)
    returned = lax.all_to_all(answers, "expert", split_axis=0, concat_axis=0, tiled=True)
    return pl.pallas_call(
        mix_kernel,
        out_shape=jax.ShapeDtypeStruct((tok_rows, width), jnp.bfloat16),
        scratch_shapes=[pltpu.VMEM((experts * PAD, CHUNK), jnp.float32)],
        name="mix",
    )(hidden_in, weights, returned)


def solution(mesh):
    placed = (
        P(("expert", "hidden"), None),
        P(),
        P(),
        P(("expert", "hidden"), None),
        P("expert", None, "hidden"),
        P("expert", None, "hidden"),
        P("expert", "hidden", None),
    )

    return jax.shard_map(
        per_device,
        mesh=mesh,
        in_specs=placed,
        out_specs=P(("expert", "hidden"), None),
        check_vma=False,
    )
```

```python
import functools

import jax
import jax.numpy as jnp
from jax import lax
from jax.experimental import pallas as pl
from jax.experimental.pallas import tpu as pltpu
from jax.sharding import PartitionSpec as P


RING = 4


PAD = 8
CHUNK = 512
MIX = 1024
TILE = 16


def slots(ids_ref):
    first, second = ids_ref[0:1, :], ids_ref[1:2, :]
    tokens = first.shape[1]
    down = lax.broadcasted_iota(jnp.int32, (tokens, tokens), 0)
    across = lax.broadcasted_iota(jnp.int32, (tokens, tokens), 1)

    def column(row):
        return jnp.sum(jnp.where(down == across, row, 0), axis=1, keepdims=True)

    first_col, second_col = column(first), column(second)
    here = lax.axis_index("expert")
    found = []
    for ids, extra in ((first, 0), (second, (first == second).astype(jnp.int32))):
        same = (first_col == ids).astype(jnp.int32) + (second_col == ids).astype(jnp.int32)
        rank = jnp.sum(jnp.where(down < across, same, 0), axis=0, keepdims=True) + extra
        offset = ((ids >> 1) - (here >> 1)) & (RING - 1)
        place = jnp.where(offset == 0, 0, jnp.where(offset == RING - 1, 1, offset + 1))
        found.append((place, (ids & 1) ^ (here & 1), rank))
    return found


def route_kernel(hidden_ref, gain_ref, ids_ref, same_ref, other_ref, normed_ref):
    count, capacity, width = same_ref.shape
    tokens = hidden_ref.shape[0]
    values = hidden_ref[...].astype(jnp.float32)
    factor = lax.rsqrt(jnp.sum(values * values, axis=1, keepdims=True) / width + 1e-05)
    normed_ref[...] = (values * factor * gain_ref[...]).astype(jnp.bfloat16)
    first, second = [(core * count + place) * PAD + rank for place, core, rank in slots(ids_ref)]
    row = lax.broadcasted_iota(jnp.int32, (2 * count * PAD, tokens), 0)
    pick = jnp.where((row == first) | (row == second), 1.0, 0.0).astype(jnp.bfloat16)

    @pl.loop(0, width // CHUNK)
    def _(step):
        columns = pl.ds(pl.multiple_of(step * CHUNK, CHUNK), CHUNK)
        rows = jnp.dot(pick, normed_ref[:, columns], preferred_element_type=jnp.float32)
        for i in range(count):
            for core, out_ref in ((0, same_ref), (1, other_ref)):
                start = (core * count + i) * PAD
                out_ref[i, :, columns] = rows[start : start + capacity].astype(jnp.bfloat16)


def gate_kernel(capacity, normed_ref, router_ref, ids_ref, out_ref):
    logits = lax.dot_general(
        router_ref[...], normed_ref[...], (((1,), (1,)), ((), ())), preferred_element_type=jnp.float32
    )
    expert = lax.broadcasted_iota(jnp.int32, logits.shape, 0)
    chosen = [
        jnp.sum(jnp.where(expert == ids_ref[k : k + 1, :], logits, 0.0), axis=0, keepdims=True)
        for k in range(2)
    ]
    gate = 1.0 / (1.0 + jnp.exp(chosen[1] - chosen[0]))
    first, second = [
        jnp.where(core == 0, place * TILE, RING * TILE + place * capacity) + rank
        for place, core, rank in slots(ids_ref)
    ]
    row = lax.broadcasted_iota(jnp.int32, out_ref.shape[1:], 0)
    rest = jnp.where(row == first, gate, 0.0) + jnp.where(row == second, 1.0 - gate, 0.0)
    for term in range(3):
        part = rest.astype(jnp.bfloat16)
        out_ref[term] = part
        rest = rest - part.astype(jnp.float32)


def mix_kernel(hidden_ref, weight_ref, own_ref, below_ref, above_ref, across_ref, other_ref, out_ref, held_ref):
    width = hidden_ref.shape[1]
    held_ref[...] = jnp.zeros_like(held_ref)
    for i, ref in enumerate((own_ref, below_ref, above_ref, across_ref, other_ref)):
        held_ref[i * TILE : i * TILE + ref.shape[0], :] = ref[...]
    weights = [weight_ref[term] for term in range(3)]

    @pl.loop(0, width // MIX)
    def _(step):
        columns = pl.ds(pl.multiple_of(step * MIX, MIX), MIX)
        rows = held_ref[:, columns]
        total = 0.0
        for weight in weights[::-1]:
            total = total + lax.dot_general(
                weight, rows, (((0,), (0,)), ((), ())), preferred_element_type=jnp.float32
            )
        out_ref[:, columns] = (hidden_ref[:, columns].astype(jnp.float32) + total).astype(jnp.bfloat16)


def along_x(value, step):
    pairs = [(2 * x + c, 2 * ((x + step) % RING) + c) for x in range(RING) for c in range(2)]
    return lax.ppermute(value, "expert", pairs)


def other_core(value):
    return lax.ppermute(value, "expert", [(i, i ^ 1) for i in range(2 * RING)])


def shift(value, axis, step):
    def target(i):
        z, y = divmod(i, RING)
        return ((z + step) % RING) * RING + y if axis == "z" else z * RING + (y + step) % RING

    return lax.ppermute(value, "hidden", [(i, target(i)) for i in range(RING * RING)])


def gather_ring(own, first, second):
    half = own.shape[1] // 2
    below, above = shift(own, first, 1), shift(own, first, -1)
    across = [shift(below[:, :half], first, 1), shift(above[:, half:], first, -1)]
    mine = jnp.concatenate([own, below, above, jnp.concatenate(across, axis=1)], axis=0)
    mine = lax.optimization_barrier(mine)
    rows = mine.shape[0] // 2
    below, above = shift(mine, second, 1), shift(mine, second, -1)
    far = [shift(below[:rows], second, 1), shift(above[rows:], second, -1)]
    return [mine], [below, above], far


def add(*terms):
    total = terms[0].astype(jnp.float32)
    for term in terms[1:]:
        total = total + term.astype(jnp.float32)
    return total.astype(jnp.bfloat16)


def spread(value, top, left, like):
    rows, columns = like.shape
    pads = (top, rows - top - value.shape[0]), (left, columns - left - value.shape[1])
    return jnp.pad(value, pads)


def reduce_rings(stages, down, orders, rows):
    half = down.shape[1] // 2
    group = RING * rows
    both = range(2)

    def product(blocks):
        value = jnp.concatenate(blocks, axis=0)
        value = jnp.dot(value, down, preferred_element_type=jnp.float32)
        return lax.optimization_barrier(value.astype(jnp.bfloat16))

    def flat(value):
        return value.reshape(-1, value.shape[-1])

    def send(blocks):
        return [
            (shift(block[:, :half], orders[i][0], 1), shift(block[:, half:], orders[i][0], -1))
            for i, block in enumerate(blocks)
        ]

    value = product([flat(stages[0][:, :, 3]), flat(stages[1][:, :, 3])])
    early = send(
        [
            jnp.concatenate(
                [value[i * rows : (i + 1) * rows], value[2 * (i + 1) * rows : 2 * (i + 2) * rows]], axis=0
            )
            for i in both
        ]
    )
    value = product([flat(stages[2][:, :, 3])])
    late = send([value[i * rows : (i + 1) * rows] for i in both])
    outer = [product([flat(act[i, :, 1:3]) for act in stages]).reshape(RING, 2, rows, -1) for i in both]
    kept = product([flat(act[:, :, 0]) for act in stages])
    results = []
    for i in both:
        first, second = orders[i]
        below, above = [outer[i][:, k].reshape(group, -1) for k in range(2)]
        above = add(above, spread(early[i][0], 0, 0, above), spread(late[i][0], 3 * rows, 0, above))
        below = add(below, spread(early[i][1], 0, half, below), spread(late[i][1], 3 * rows, half, below))
        above, below = shift(above, first, 1), shift(below, first, -1)
        own = [
            kept[i * rows : (i + 1) * rows],
            kept[2 * (i + 1) * rows : 2 * (i + 2) * rows],
            kept[(6 + i) * rows : (7 + i) * rows],
        ]
        own = add(jnp.concatenate(own, axis=0), above, below)
        across = own[3 * rows :]
        low = shift(across[:, :half], second, 1)
        high = shift(across[:, half:], second, -1)
        above, below = own[2 * rows : 3 * rows], own[rows : 2 * rows]
        above = shift(add(above, spread(low, 0, 0, above)), second, 1)
        below = shift(add(below, spread(high, 0, half, below)), second, -1)
        results.append(add(own[:rows], above, below))
    return results


def per_device(hidden_in, norm_gain, router_weight, expert_ids, gate_proj, up_proj, down_proj):
    experts = lax.axis_size("expert")
    tok_rows = hidden_in.shape[0]
    width = hidden_in.shape[1]
    top_count = expert_ids.shape[1]
    capacity = 3 * tok_rows * top_count // (2 * experts)
    rows = experts * capacity
    ids = expert_ids.T
    piece = jax.ShapeDtypeStruct((RING, capacity, width), jnp.bfloat16)
    same, other, normed = pl.pallas_call(
        route_kernel,
        out_shape=(piece, piece, jax.ShapeDtypeStruct((tok_rows, width), jnp.bfloat16)),
        name="route",
    )(hidden_in, norm_gain.reshape(1, width), ids)
    weights = pl.pallas_call(
        functools.partial(gate_kernel, capacity),
        out_shape=jax.ShapeDtypeStruct((3, (RING + 2) * TILE, tok_rows), jnp.bfloat16),
        name="gates",
    )(normed, router_weight.T, ids)
    gate_local = gate_proj[0]
    up_local = up_proj[0]
    down_local = down_proj[0]
    other = other_core(other)
    both = [jnp.concatenate([same[i], other[i]], axis=0) for i in range(RING)]
    arrived = [
        jnp.concatenate([both[0], along_x(both[2], 1)], axis=0),
        jnp.concatenate([along_x(both[1], -1), along_x(both[3], 2)], axis=0),
    ]
    arrived = [lax.optimization_barrier(value) for value in arrived]
    part = rows // 2
    orders = (("z", "y"), ("y", "z"))
    gathered = [gather_ring(arrived[i], *orders[i]) for i in range(2)]
    stages = []
    for stage in range(3):
        value = jnp.concatenate(gathered[0][stage] + gathered[1][stage], axis=0)
        gate = jnp.dot(value, gate_local, preferred_element_type=jnp.float32)
        upper = jnp.dot(value, up_local, preferred_element_type=jnp.float32)
        act = (jax.nn.silu(gate) * upper).astype(jnp.bfloat16)
        stages.append(act.reshape(2, -1, RING, part, act.shape[1]))
    answers = reduce_rings(stages, down_local, orders, part)
    half = part // 2
    back = [
        answers[0][:half],
        along_x(answers[1][:half], 1),
        along_x(answers[0][half:], -1),
        along_x(answers[1][half:], 2),
    ]
    crossed = other_core(jnp.concatenate([value[capacity:] for value in back], axis=0))
    return pl.pallas_call(
        mix_kernel,
        out_shape=jax.ShapeDtypeStruct((tok_rows, width), jnp.bfloat16),
        scratch_shapes=[pltpu.VMEM(((RING + 2) * TILE, width), jnp.bfloat16)],
        name="mix",
    )(hidden_in, weights, *back, crossed)


def solution(mesh):
    placed = (
        P(("expert", "hidden"), None),
        P(),
        P(),
        P(("expert", "hidden"), None),
        P("expert", None, "hidden"),
        P("expert", None, "hidden"),
        P("expert", "hidden", None),
    )

    return jax.shard_map(
        per_device,
        mesh=mesh,
        in_specs=placed,
        out_specs=P(("expert", "hidden"), None),
        check_vma=False,
    )
```

```python
import functools

import jax
import jax.numpy as jnp
from jax import lax
from jax.experimental import pallas as pl
from jax.experimental.pallas import tpu as pltpu
from jax.sharding import PartitionSpec as P


RING = 4


PAD = 8
CHUNK = 512
MIX = 1024


def slots(ids_ref):
    first, second = ids_ref[0:1, :], ids_ref[1:2, :]
    tokens = first.shape[1]
    down = lax.broadcasted_iota(jnp.int32, (tokens, tokens), 0)
    across = lax.broadcasted_iota(jnp.int32, (tokens, tokens), 1)

    def column(row):
        return jnp.sum(jnp.where(down == across, row, 0), axis=1, keepdims=True)

    first_col, second_col = column(first), column(second)
    here = lax.axis_index("expert")
    found = []
    for ids, extra in ((first, 0), (second, (first == second).astype(jnp.int32))):
        same = (first_col == ids).astype(jnp.int32) + (second_col == ids).astype(jnp.int32)
        rank = jnp.sum(jnp.where(down < across, same, 0), axis=0, keepdims=True) + extra
        offset = ((ids >> 1) - (here >> 1)) & (RING - 1)
        place = jnp.where(offset == 0, 0, jnp.where(offset == RING - 1, 1, offset + 1))
        found.append((place, (ids & 1) ^ (here & 1), rank))
    return found


def route_kernel(hidden_ref, gain_ref, ids_ref, same_ref, other_ref, normed_ref):
    count, capacity, width = same_ref.shape
    tokens = hidden_ref.shape[0]
    values = hidden_ref[...].astype(jnp.float32)
    factor = lax.rsqrt(jnp.sum(values * values, axis=1, keepdims=True) / width + 1e-05)
    normed_ref[...] = (values * factor * gain_ref[...]).astype(jnp.bfloat16)
    first, second = [(core * count + place) * PAD + rank for place, core, rank in slots(ids_ref)]
    row = lax.broadcasted_iota(jnp.int32, (2 * count * PAD, tokens), 0)
    pick = jnp.where((row == first) | (row == second), 1.0, 0.0).astype(jnp.bfloat16)

    @pl.loop(0, width // CHUNK)
    def _(step):
        columns = pl.ds(pl.multiple_of(step * CHUNK, CHUNK), CHUNK)
        rows = jnp.dot(pick, normed_ref[:, columns], preferred_element_type=jnp.float32)
        for i in range(count):
            for core, out_ref in ((0, same_ref), (1, other_ref)):
                start = (core * count + i) * PAD
                out_ref[i, :, columns] = rows[start : start + capacity].astype(jnp.bfloat16)


def gate_kernel(capacity, normed_ref, router_ref, ids_ref, out_ref):
    logits = lax.dot_general(
        router_ref[...], normed_ref[...], (((1,), (1,)), ((), ())), preferred_element_type=jnp.float32
    )
    expert = lax.broadcasted_iota(jnp.int32, logits.shape, 0)
    chosen = [
        jnp.sum(jnp.where(expert == ids_ref[k : k + 1, :], logits, 0.0), axis=0, keepdims=True)
        for k in range(2)
    ]
    gate = 1.0 / (1.0 + jnp.exp(chosen[1] - chosen[0]))
    found = slots(ids_ref)
    row = lax.broadcasted_iota(jnp.int32, out_ref.shape[2:], 0)
    for half in range(2):
        first, second = [
            (core * RING + place) * 4 * capacity + (2 * half + core) * capacity + rank
            for place, core, rank in found
        ]
        rest = jnp.where(row == first, gate, 0.0) + jnp.where(row == second, 1.0 - gate, 0.0)
        for term in range(3):
            part = rest.astype(jnp.bfloat16)
            out_ref[half, term] = part
            rest = rest - part.astype(jnp.float32)


def mix_kernel(hidden_ref, weight_ref, own_ref, below_ref, above_ref, across_ref, other_ref, out_ref, held_ref):
    half = held_ref.shape[1]
    start = 0
    for ref in (own_ref, below_ref, above_ref, across_ref, other_ref):
        held_ref[start : start + ref.shape[0], :] = ref[...]
        start += ref.shape[0]

    @pl.loop(0, half // MIX)
    def _(step):
        rows = held_ref[:, pl.ds(pl.multiple_of(step * MIX, MIX), MIX)]
        for side in range(2):
            columns = pl.ds(pl.multiple_of(side * half + step * MIX, MIX), MIX)
            total = hidden_ref[:, columns].astype(jnp.float32)
            mixed = 0.0
            for term in (2, 1, 0):
                mixed = mixed + lax.dot_general(
                    weight_ref[side, term],
                    rows,
                    (((0,), (0,)), ((), ())),
                    preferred_element_type=jnp.float32,
                )
            out_ref[:, columns] = (total + mixed).astype(jnp.bfloat16)


def along_x(value, step):
    pairs = [(2 * x + c, 2 * ((x + step) % RING) + c) for x in range(RING) for c in range(2)]
    return lax.ppermute(value, "expert", pairs)


def other_core(value):
    return lax.ppermute(value, "expert", [(i, i ^ 1) for i in range(2 * RING)])


def shift(value, axis, step):
    def target(i):
        z, y = divmod(i, RING)
        return ((z + step) % RING) * RING + y if axis == "z" else z * RING + (y + step) % RING

    return lax.ppermute(value, "hidden", [(i, target(i)) for i in range(RING * RING)])


def gather_ring(own, first, second):
    half = own.shape[1] // 2
    below, above = shift(own, first, 1), shift(own, first, -1)
    across = [shift(below[:, :half], first, 1), shift(above[:, half:], first, -1)]
    mine = jnp.concatenate([own, below, above, jnp.concatenate(across, axis=1)], axis=0)
    mine = lax.optimization_barrier(mine)
    rows = mine.shape[0] // 2
    below, above = shift(mine, second, 1), shift(mine, second, -1)
    far = [shift(below[:rows], second, 1), shift(above[rows:], second, -1)]
    return [mine], [below, above], far


def add(*terms):
    total = terms[0].astype(jnp.float32)
    for term in terms[1:]:
        total = total + term.astype(jnp.float32)
    return total.astype(jnp.bfloat16)


def reduce_rings(stages, down, orders, rows):
    start, middle, end = stages
    both = range(2)

    def product(blocks):
        value = [block.reshape(-1, block.shape[-1]) for block in blocks]
        value = jnp.dot(jnp.concatenate(value, axis=0), down, preferred_element_type=jnp.float32)
        return lax.optimization_barrier(value.astype(jnp.bfloat16))

    def piece(value, base, count):
        return value[base * rows : (base + count) * rows]

    early = product([middle[:, :, 1:].swapaxes(1, 2), start[:, 0, 3]])
    down_one = [
        shift(jnp.concatenate([piece(early, 12 + i, 1), piece(early, 6 * i, 2)], axis=0), orders[i][0], -1)
        for i in both
    ]
    up_one = [shift(piece(early, 6 * i + 4, 2), orders[i][0], 1) for i in both]
    late = product([end[:, 0, 1:], start[:, 0, 1:3]])
    down_two = [shift(piece(late, 3 * i + 2, 1), orders[i][0], -1) for i in both]
    up_two = [
        shift(jnp.concatenate([piece(late, 7 + 2 * i, 1), piece(late, 3 * i + 1, 1)], axis=0), orders[i][0], 1)
        for i in both
    ]
    up_sum = [add(piece(early, 6 * i + 2, 2), up_one[i]) for i in both]
    down_sum = [
        jnp.concatenate(
            [add(piece(late, 6 + 2 * i, 1), down_one[i][:rows]), add(piece(late, 3 * i, 1), down_two[i])], axis=0
        )
        for i in both
    ]
    up_three = [shift(up_sum[i], orders[i][0], 1) for i in both]
    down_three = [shift(down_sum[i], orders[i][0], -1) for i in both]
    kept = [product([start[i, 0, 0], end[i, 0, 0], middle[i, :, 0]]) for i in both]
    results = []
    for i in both:
        second = orders[i][1]
        half = down.shape[1] // 2
        outer = add(kept[i][: 2 * rows], up_two[i], down_three[i])
        inner = add(kept[i][2 * rows :], up_three[i], down_one[i][rows:])
        own, across = outer[:rows], outer[rows:]
        below, above = inner[:rows], inner[rows:]
        low = shift(across[:, :half], second, 1)
        high = shift(across[:, half:], second, -1)
        above = jnp.concatenate([add(above[:, :half], low), above[:, half:]], axis=1)
        below = jnp.concatenate([below[:, :half], add(below[:, half:], high)], axis=1)
        results.append(add(own, shift(above, second, 1), shift(below, second, -1)))
    return results


def pack(value):
    half = value.shape[1] // 2
    return jnp.concatenate([value[:, :half], value[:, half:]], axis=0)


def unpack(value):
    half = value.shape[0] // 2
    return jnp.concatenate([value[:half], value[half:]], axis=1)


def per_device(hidden_in, norm_gain, router_weight, expert_ids, gate_proj, up_proj, down_proj):
    experts = lax.axis_size("expert")
    tok_rows = hidden_in.shape[0]
    width = hidden_in.shape[1]
    top_count = expert_ids.shape[1]
    capacity = 3 * tok_rows * top_count // (2 * experts)
    rows = experts * capacity
    ids = expert_ids.T
    piece = jax.ShapeDtypeStruct((RING, capacity, width), jnp.bfloat16)
    same, other, normed = pl.pallas_call(
        route_kernel,
        out_shape=(piece, piece, jax.ShapeDtypeStruct((tok_rows, width), jnp.bfloat16)),
        compiler_params=pltpu.CompilerParams(vmem_limit_bytes=8 * 1024 * 1024),
        name="route",
    )(hidden_in, norm_gain.reshape(1, width), ids)
    weights = pl.pallas_call(
        functools.partial(gate_kernel, capacity),
        out_shape=jax.ShapeDtypeStruct((2, 3, 8 * RING * capacity, tok_rows), jnp.bfloat16),
        compiler_params=pltpu.CompilerParams(vmem_limit_bytes=4 * 1024 * 1024),
    name="gates",
    )(normed, router_weight.T, ids)
    gate_local = gate_proj[0]
    up_local = up_proj[0]
    down_local = down_proj[0]
    other = other_core(other)
    both = [jnp.concatenate([same[i], other[i]], axis=0) for i in range(RING)]
    moved = [unpack(along_x(pack(both[i]), step)) for i, step in ((2, 1), (1, -1), (3, 2))]
    arrived = [jnp.concatenate([both[0], moved[0]], axis=0), jnp.concatenate(moved[1:], axis=0)]
    arrived = [lax.optimization_barrier(value) for value in arrived]
    part = rows // 2
    orders = (("z", "y"), ("y", "z"))
    gathered = [gather_ring(arrived[i], *orders[i]) for i in range(2)]
    stages = []
    for stage in range(3):
        value = jnp.concatenate(gathered[0][stage] + gathered[1][stage], axis=0)
        gate = jnp.dot(value, gate_local, preferred_element_type=jnp.float32)
        upper = jnp.dot(value, up_local, preferred_element_type=jnp.float32)
        act = (jax.nn.silu(gate) * upper).astype(jnp.bfloat16)
        stages.append(act.reshape(2, -1, RING, part, act.shape[1]))
    answers = reduce_rings(stages, down_local, orders, part)
    half = part // 2
    back = [
        pack(answers[0][:half]),
        along_x(pack(answers[1][:half]), 1),
        along_x(pack(answers[0][half:]), -1),
        along_x(pack(answers[1][half:]), 2),
    ]
    back[0] = lax.optimization_barrier(back[0])
    crossed = other_core(jnp.concatenate(back, axis=0))
    return pl.pallas_call(
        mix_kernel,
        out_shape=jax.ShapeDtypeStruct((tok_rows, width), jnp.bfloat16),
        scratch_shapes=[pltpu.VMEM((8 * RING * capacity, width // 2), jnp.bfloat16)],
        compiler_params=pltpu.CompilerParams(vmem_limit_bytes=8 * 1024 * 1024),
        name="mix",
    )(hidden_in, weights, *back, crossed)


def solution(mesh):
    placed = (
        P(("expert", "hidden"), None),
        P(),
        P(),
        P(("expert", "hidden"), None),
        P("expert", None, "hidden"),
        P("expert", None, "hidden"),
        P("expert", "hidden", None),
    )

    return jax.shard_map(
        per_device,
        mesh=mesh,
        in_specs=placed,
        out_specs=P(("expert", "hidden"), None),
        check_vma=False,
    )
```

```python
import functools

import jax
import jax.numpy as jnp
from jax import lax
from jax.experimental import pallas as pl
from jax.experimental.pallas import tpu as pltpu
from jax.sharding import PartitionSpec as P


RING = 4


PAD = 8
CHUNK = 512
MIX = 1024


def slots(ids_ref):
    first, second = ids_ref[0:1, :], ids_ref[1:2, :]
    tokens = first.shape[1]
    down = lax.broadcasted_iota(jnp.int32, (tokens, tokens), 0)
    across = lax.broadcasted_iota(jnp.int32, (tokens, tokens), 1)

    def column(row):
        return jnp.sum(jnp.where(down == across, row, 0), axis=1, keepdims=True)

    first_col, second_col = column(first), column(second)
    here = lax.axis_index("expert")
    found = []
    for ids, extra in ((first, 0), (second, (first == second).astype(jnp.int32))):
        same = (first_col == ids).astype(jnp.int32) + (second_col == ids).astype(jnp.int32)
        rank = jnp.sum(jnp.where(down < across, same, 0), axis=0, keepdims=True) + extra
        offset = ((ids >> 1) - (here >> 1)) & (RING - 1)
        place = jnp.where(offset == 0, 0, jnp.where(offset == RING - 1, 1, offset + 1))
        found.append((place, (ids & 1) ^ (here & 1), rank))
    return found


def route_kernel(hidden_ref, gain_ref, ids_ref, same_ref, other_ref, normed_ref):
    count, capacity, width = same_ref.shape
    tokens = hidden_ref.shape[0]
    values = hidden_ref[...].astype(jnp.float32)
    factor = lax.rsqrt(jnp.sum(values * values, axis=1, keepdims=True) / width + 1e-05)
    normed_ref[...] = (values * factor * gain_ref[...]).astype(jnp.bfloat16)
    first, second = [(core * count + place) * PAD + rank for place, core, rank in slots(ids_ref)]
    row = lax.broadcasted_iota(jnp.int32, (2 * count * PAD, tokens), 0)
    pick = jnp.where((row == first) | (row == second), 1.0, 0.0).astype(jnp.bfloat16)

    @pl.loop(0, width // CHUNK)
    def _(step):
        columns = pl.ds(pl.multiple_of(step * CHUNK, CHUNK), CHUNK)
        rows = jnp.dot(pick, normed_ref[:, columns], preferred_element_type=jnp.float32)
        for i in range(count):
            for core, out_ref in ((0, same_ref), (1, other_ref)):
                start = (core * count + i) * PAD
                out_ref[i, :, columns] = rows[start : start + capacity].astype(jnp.bfloat16)


def gate_kernel(capacity, normed_ref, router_ref, ids_ref, out_ref):
    logits = lax.dot_general(
        router_ref[...], normed_ref[...], (((1,), (1,)), ((), ())), preferred_element_type=jnp.float32
    )
    expert = lax.broadcasted_iota(jnp.int32, logits.shape, 0)
    chosen = [
        jnp.sum(jnp.where(expert == ids_ref[k : k + 1, :], logits, 0.0), axis=0, keepdims=True)
        for k in range(2)
    ]
    gate = 1.0 / (1.0 + jnp.exp(chosen[1] - chosen[0]))
    found = slots(ids_ref)
    row = lax.broadcasted_iota(jnp.int32, out_ref.shape[2:], 0)
    for half in range(2):
        first, second = [
            (core * RING + place) * 4 * capacity + (2 * half + core) * capacity + rank
            for place, core, rank in found
        ]
        rest = jnp.where(row == first, gate, 0.0) + jnp.where(row == second, 1.0 - gate, 0.0)
        for term in range(3):
            part = rest.astype(jnp.bfloat16)
            out_ref[half, term] = part
            rest = rest - part.astype(jnp.float32)


def mix_kernel(hidden_ref, weight_ref, own_ref, below_ref, above_ref, across_ref, other_ref, out_ref, held_ref):
    half = held_ref.shape[1]
    start = 0
    for ref in (own_ref, below_ref, above_ref, across_ref, other_ref):
        held_ref[start : start + ref.shape[0], :] = ref[...]
        start += ref.shape[0]

    @pl.loop(0, half // MIX)
    def _(step):
        rows = held_ref[:, pl.ds(pl.multiple_of(step * MIX, MIX), MIX)]
        for side in range(2):
            columns = pl.ds(pl.multiple_of(side * half + step * MIX, MIX), MIX)
            total = hidden_ref[:, columns].astype(jnp.float32)
            mixed = 0.0
            for term in (2, 1, 0):
                mixed = mixed + lax.dot_general(
                    weight_ref[side, term],
                    rows,
                    (((0,), (0,)), ((), ())),
                    preferred_element_type=jnp.float32,
                )
            out_ref[:, columns] = (total + mixed).astype(jnp.bfloat16)


def along_x(value, step):
    pairs = [(2 * x + c, 2 * ((x + step) % RING) + c) for x in range(RING) for c in range(2)]
    return lax.ppermute(value, "expert", pairs)


def other_core(value):
    return lax.ppermute(value, "expert", [(i, i ^ 1) for i in range(2 * RING)])


def shift(value, axis, step):
    def target(i):
        z, y = divmod(i, RING)
        return ((z + step) % RING) * RING + y if axis == "z" else z * RING + (y + step) % RING

    return lax.ppermute(value, "hidden", [(i, target(i)) for i in range(RING * RING)])


def gather_ring(own, first, second):
    half = own.shape[1] // 2
    below, above = shift(own, first, 1), shift(own, first, -1)
    across = [shift(below[:, :half], first, 1), shift(above[:, half:], first, -1)]
    near = lax.optimization_barrier(jnp.concatenate([own, below, above], axis=0))
    far = jnp.concatenate(across, axis=1)
    rows = own.shape[0]
    below = [shift(near, second, 1), shift(far, second, 1)]
    above = [shift(near, second, -1), shift(far, second, -1)]
    last = [
        shift(below[0][: 2 * rows], second, 1),
        shift(jnp.concatenate([above[0][2 * rows :], above[1]], axis=0), second, -1),
    ]
    return [near, far], below + above, last


def add(*terms):
    total = terms[0].astype(jnp.float32)
    for term in terms[1:]:
        total = total + term.astype(jnp.float32)
    return total.astype(jnp.bfloat16)


def reduce_rings(stages, down, orders, rows):
    start, middle, end = stages
    both = range(2)

    def product(blocks):
        value = [block.reshape(-1, block.shape[-1]) for block in blocks]
        value = jnp.dot(jnp.concatenate(value, axis=0), down, preferred_element_type=jnp.float32)
        return lax.optimization_barrier(value.astype(jnp.bfloat16))

    def piece(value, base, count):
        return value[base * rows : (base + count) * rows]

    early = product([middle[:, :, 1:].swapaxes(1, 2), start[:, 0, 2:]])
    up_one = [shift(piece(early, 6 * i + 4, 2), orders[i][0], 1) for i in both]
    down_one = [
        shift(jnp.concatenate([piece(early, 13 + 2 * i, 1), piece(early, 6 * i, 2)], axis=0), orders[i][0], -1)
        for i in both
    ]
    up_own = [shift(piece(early, 12 + 2 * i, 1), orders[i][0], 1) for i in both]
    late = product([end[:, 0, 1:], start[:, 0, 1]])
    down_two = [shift(piece(late, 3 * i + 2, 1), orders[i][0], -1) for i in both]
    up_sum = [add(piece(early, 6 * i + 2, 2), up_one[i]) for i in both]
    up_three = [shift(up_sum[i], orders[i][0], 1) for i in both]
    up_two = [shift(piece(late, 3 * i + 1, 1), orders[i][0], 1) for i in both]
    down_sum = [
        jnp.concatenate(
            [add(piece(late, 6 + i, 1), down_one[i][:rows]), add(piece(late, 3 * i, 1), down_two[i])], axis=0
        )
        for i in both
    ]
    down_three = [shift(down_sum[i], orders[i][0], -1) for i in both]
    kept = [product([start[i, 0, 0], end[i, 0, 0], middle[i, :, 0]]) for i in both]
    sides = []
    for i in both:
        inner = add(kept[i][2 * rows :], up_three[i], down_one[i][rows:])
        sides.append((shift(inner[rows:], orders[i][1], 1), shift(inner[:rows], orders[i][1], -1)))
    results = []
    for i in both:
        across = add(kept[i][rows : 2 * rows], up_two[i], down_three[i][rows:])
        across = shift(across, orders[i][1], 2)
        own = lax.optimization_barrier(add(kept[i][:rows], up_own[i], down_three[i][:rows]))
        results.append(add(own, *sides[i], across))
    return results


def pack(value):
    half = value.shape[1] // 2
    return jnp.concatenate([value[:, :half], value[:, half:]], axis=0)


def unpack(value):
    half = value.shape[0] // 2
    return jnp.concatenate([value[:half], value[half:]], axis=1)


def per_device(hidden_in, norm_gain, router_weight, expert_ids, gate_proj, up_proj, down_proj):
    experts = lax.axis_size("expert")
    tok_rows = hidden_in.shape[0]
    width = hidden_in.shape[1]
    top_count = expert_ids.shape[1]
    capacity = 3 * tok_rows * top_count // (2 * experts)
    rows = experts * capacity
    ids = expert_ids.T
    piece = jax.ShapeDtypeStruct((RING, capacity, width), jnp.bfloat16)
    same, other, normed = pl.pallas_call(
        route_kernel,
        out_shape=(piece, piece, jax.ShapeDtypeStruct((tok_rows, width), jnp.bfloat16)),
        compiler_params=pltpu.CompilerParams(vmem_limit_bytes=8 * 1024 * 1024),
        name="route",
    )(hidden_in, norm_gain.reshape(1, width), ids)
    weights = pl.pallas_call(
        functools.partial(gate_kernel, capacity),
        out_shape=jax.ShapeDtypeStruct((2, 3, 8 * RING * capacity, tok_rows), jnp.bfloat16),
        compiler_params=pltpu.CompilerParams(vmem_limit_bytes=4 * 1024 * 1024),
    name="gates",
    )(normed, router_weight.T, ids)
    gate_local = gate_proj[0]
    up_local = up_proj[0]
    down_local = down_proj[0]
    other = other_core(other)
    both = [jnp.concatenate([same[i], other[i]], axis=0) for i in range(RING)]
    moved = [unpack(along_x(pack(both[i]), step)) for i, step in ((2, 1), (1, -1), (3, 2))]
    arrived = [jnp.concatenate([both[0], moved[0]], axis=0), jnp.concatenate(moved[1:], axis=0)]
    arrived = [lax.optimization_barrier(value) for value in arrived]
    part = rows // 2
    orders = (("z", "y"), ("y", "z"))
    gathered = [gather_ring(arrived[i], *orders[i]) for i in range(2)]
    stages = []
    for stage in range(3):
        value = jnp.concatenate(gathered[0][stage] + gathered[1][stage], axis=0)
        gate = jnp.dot(value, gate_local, preferred_element_type=jnp.float32)
        upper = jnp.dot(value, up_local, preferred_element_type=jnp.float32)
        act = (jax.nn.silu(gate) * upper).astype(jnp.bfloat16)
        stages.append(act.reshape(2, -1, RING, part, act.shape[1]))
    answers = reduce_rings(stages, down_local, orders, part)
    half = part // 2
    back = [
        pack(answers[0][:half]),
        along_x(pack(answers[1][:half]), 1),
        along_x(pack(answers[0][half:]), -1),
        along_x(pack(answers[1][half:]), 2),
    ]
    back[0] = lax.optimization_barrier(back[0])
    crossed = other_core(jnp.concatenate(back, axis=0))
    return pl.pallas_call(
        mix_kernel,
        out_shape=jax.ShapeDtypeStruct((tok_rows, width), jnp.bfloat16),
        scratch_shapes=[pltpu.VMEM((8 * RING * capacity, width // 2), jnp.bfloat16)],
        compiler_params=pltpu.CompilerParams(vmem_limit_bytes=8 * 1024 * 1024),
        name="mix",
    )(hidden_in, weights, *back, crossed)


def solution(mesh):
    placed = (
        P(("expert", "hidden"), None),
        P(),
        P(),
        P(("expert", "hidden"), None),
        P("expert", None, "hidden"),
        P("expert", None, "hidden"),
        P("expert", "hidden", None),
    )

    return jax.shard_map(
        per_device,
        mesh=mesh,
        in_specs=placed,
        out_specs=P(("expert", "hidden"), None),
        check_vma=False,
    )
```

```python
import functools

import jax
import jax.numpy as jnp
from jax import lax
from jax.experimental import pallas as pl
from jax.experimental.pallas import tpu as pltpu
from jax.sharding import PartitionSpec as P


RING = 4


PAD = 8
CHUNK = 512
MIX = 1024


def slots(ids_ref):
    first, second = ids_ref[0:1, :], ids_ref[1:2, :]
    tokens = first.shape[1]
    down = lax.broadcasted_iota(jnp.int32, (tokens, tokens), 0)
    across = lax.broadcasted_iota(jnp.int32, (tokens, tokens), 1)

    def column(row):
        return jnp.sum(jnp.where(down == across, row, 0), axis=1, keepdims=True)

    first_col, second_col = column(first), column(second)
    here = lax.axis_index("expert")
    found = []
    for ids, extra in ((first, 0), (second, (first == second).astype(jnp.int32))):
        same = (first_col == ids).astype(jnp.int32) + (second_col == ids).astype(jnp.int32)
        rank = jnp.sum(jnp.where(down < across, same, 0), axis=0, keepdims=True) + extra
        offset = ((ids >> 1) - (here >> 1)) & (RING - 1)
        place = jnp.where(offset == 0, 0, jnp.where(offset == RING - 1, 1, offset + 1))
        found.append((place, (ids & 1) ^ (here & 1), rank))
    return found


def route_kernel(
    hidden_hbm, gain_hbm, ids_hbm, same_ref, other_ref, normed_ref, hidden_ref, gain_ref, ids_ref, sems
):
    pairs = ((hidden_hbm, hidden_ref), (gain_hbm, gain_ref), (ids_hbm, ids_ref))
    copies = [pltpu.make_async_copy(source, target, sems.at[i]) for i, (source, target) in enumerate(pairs)]
    for copy in copies:
        copy.start()
    for copy in copies:
        copy.wait()
    count, capacity, width = same_ref.shape
    tokens = hidden_ref.shape[0]
    values = hidden_ref[...].astype(jnp.float32)
    factor = lax.rsqrt(jnp.sum(values * values, axis=1, keepdims=True) / width + 1e-05)
    normed_ref[...] = (values * factor * gain_ref[...]).astype(jnp.bfloat16)
    first, second = [(core * count + place) * PAD + rank for place, core, rank in slots(ids_ref)]
    row = lax.broadcasted_iota(jnp.int32, (2 * count * PAD, tokens), 0)
    pick = jnp.where((row == first) | (row == second), 1.0, 0.0).astype(jnp.bfloat16)

    @pl.loop(0, width // CHUNK)
    def _(step):
        columns = pl.ds(pl.multiple_of(step * CHUNK, CHUNK), CHUNK)
        rows = jnp.dot(pick, normed_ref[:, columns], preferred_element_type=jnp.float32)
        for i in range(count):
            for core, out_ref in ((0, same_ref), (1, other_ref)):
                start = (core * count + i) * PAD
                out_ref[i, :, columns] = rows[start : start + capacity].astype(jnp.bfloat16)


def gate_kernel(capacity, normed_ref, router_ref, ids_ref, out_ref):
    logits = lax.dot_general(
        router_ref[...], normed_ref[...], (((1,), (1,)), ((), ())), preferred_element_type=jnp.float32
    )
    expert = lax.broadcasted_iota(jnp.int32, logits.shape, 0)
    chosen = [
        jnp.sum(jnp.where(expert == ids_ref[k : k + 1, :], logits, 0.0), axis=0, keepdims=True)
        for k in range(2)
    ]
    gate = 1.0 / (1.0 + jnp.exp(chosen[1] - chosen[0]))
    found = slots(ids_ref)
    row = lax.broadcasted_iota(jnp.int32, out_ref.shape[2:], 0)
    for half in range(2):
        first, second = [
            (core * RING + place) * 4 * capacity + (2 * half + core) * capacity + rank
            for place, core, rank in found
        ]
        rest = jnp.where(row == first, gate, 0.0) + jnp.where(row == second, 1.0 - gate, 0.0)
        for term in range(3):
            part = rest.astype(jnp.bfloat16)
            out_ref[half, term] = part
            rest = rest - part.astype(jnp.float32)


def mix_kernel(hidden_ref, weight_ref, own_ref, below_ref, above_ref, across_ref, other_ref, out_ref, held_ref):
    half = held_ref.shape[1]
    start = 0
    for ref in (own_ref, below_ref, above_ref, across_ref, other_ref):
        held_ref[start : start + ref.shape[0], :] = ref[...]
        start += ref.shape[0]

    @pl.loop(0, half // MIX)
    def _(step):
        rows = held_ref[:, pl.ds(pl.multiple_of(step * MIX, MIX), MIX)]
        for side in range(2):
            columns = pl.ds(pl.multiple_of(side * half + step * MIX, MIX), MIX)
            total = hidden_ref[:, columns].astype(jnp.float32)
            mixed = 0.0
            for term in (2, 1, 0):
                mixed = mixed + lax.dot_general(
                    weight_ref[side, term],
                    rows,
                    (((0,), (0,)), ((), ())),
                    preferred_element_type=jnp.float32,
                )
            out_ref[:, columns] = (total + mixed).astype(jnp.bfloat16)


def along_x(value, step):
    pairs = [(2 * x + c, 2 * ((x + step) % RING) + c) for x in range(RING) for c in range(2)]
    return lax.ppermute(value, "expert", pairs)


def other_core(value):
    return lax.ppermute(value, "expert", [(i, i ^ 1) for i in range(2 * RING)])


def shift(value, axis, step):
    def target(i):
        z, y = divmod(i, RING)
        return ((z + step) % RING) * RING + y if axis == "z" else z * RING + (y + step) % RING

    return lax.ppermute(value, "hidden", [(i, target(i)) for i in range(RING * RING)])


def gather_ring(own, first, second):
    half = own.shape[1] // 2
    below, above = shift(own, first, 1), shift(own, first, -1)
    across = [shift(below[:, :half], first, 1), shift(above[:, half:], first, -1)]
    near = lax.optimization_barrier(jnp.concatenate([own, below, above], axis=0))
    far = jnp.concatenate(across, axis=1)
    rows = own.shape[0]
    below, above = [shift(near, second, 1)], [shift(near, second, -1)]
    below.append(shift(far, second, 1))
    above.append(shift(far, second, -1))
    last = [
        shift(below[0][: 2 * rows], second, 1),
        shift(jnp.concatenate([above[0][2 * rows :], above[1]], axis=0), second, -1),
    ]
    return [near, far], below + above, last


def add(*terms):
    total = terms[0].astype(jnp.float32)
    for term in terms[1:]:
        total = total + term.astype(jnp.float32)
    return total.astype(jnp.bfloat16)


def reduce_rings(stages, down, orders, rows):
    start, middle, end = stages
    both = range(2)

    def product(blocks):
        value = [block.reshape(-1, block.shape[-1]) for block in blocks]
        value = jnp.dot(jnp.concatenate(value, axis=0), down, preferred_element_type=jnp.float32)
        return lax.optimization_barrier(value.astype(jnp.bfloat16))

    def piece(value, base, count):
        return value[base * rows : (base + count) * rows]

    early = product([middle[:, :, 1:].swapaxes(1, 2), start[:, 0, 2:]])
    up_one = [shift(piece(early, 6 * i + 4, 2), orders[i][0], 1) for i in both]
    down_one = [
        shift(jnp.concatenate([piece(early, 13 + 2 * i, 1), piece(early, 6 * i, 2)], axis=0), orders[i][0], -1)
        for i in both
    ]
    up_own = [shift(piece(early, 12 + 2 * i, 1), orders[i][0], 1) for i in both]
    late = product([end[:, 0, 1:], start[:, 0, 1]])
    down_two = [shift(piece(late, 3 * i + 2, 1), orders[i][0], -1) for i in both]
    up_sum = [add(piece(early, 6 * i + 2, 2), up_one[i]) for i in both]
    up_three = [shift(up_sum[i], orders[i][0], 1) for i in both]
    up_two = [shift(piece(late, 3 * i + 1, 1), orders[i][0], 1) for i in both]
    down_sum = [
        jnp.concatenate(
            [add(piece(late, 6 + i, 1), down_one[i][:rows]), add(piece(late, 3 * i, 1), down_two[i])], axis=0
        )
        for i in both
    ]
    down_three = [shift(down_sum[i], orders[i][0], -1) for i in both]
    kept = [product([start[i, 0, 0], end[i, 0, 0], middle[i, :, 0]]) for i in both]
    sides = []
    for i in both:
        inner = add(kept[i][2 * rows :], up_three[i], down_one[i][rows:])
        sides.append((shift(inner[rows:], orders[i][1], 1), shift(inner[:rows], orders[i][1], -1)))
    results = []
    for i in both:
        across = add(kept[i][rows : 2 * rows], up_two[i], down_three[i][rows:])
        across = shift(across, orders[i][1], 2)
        own = lax.optimization_barrier(add(kept[i][:rows], up_own[i], down_three[i][:rows]))
        results.append(add(own, *sides[i], across))
    return results


def pack(value):
    half = value.shape[1] // 2
    return jnp.concatenate([value[:, :half], value[:, half:]], axis=0)


def unpack(value):
    half = value.shape[0] // 2
    return jnp.concatenate([value[:half], value[half:]], axis=1)


def per_device(hidden_in, norm_gain, router_weight, expert_ids, gate_proj, up_proj, down_proj):
    experts = lax.axis_size("expert")
    tok_rows = hidden_in.shape[0]
    width = hidden_in.shape[1]
    top_count = expert_ids.shape[1]
    capacity = 3 * tok_rows * top_count // (2 * experts)
    rows = experts * capacity
    ids = expert_ids.T
    piece = jax.ShapeDtypeStruct((RING, capacity, width), jnp.bfloat16)
    same, other, normed = pl.pallas_call(
        route_kernel,
        out_shape=(piece, piece, jax.ShapeDtypeStruct((tok_rows, width), jnp.bfloat16)),
        in_specs=[pl.BlockSpec(memory_space=pltpu.HBM)] * 3,
        scratch_shapes=[
            pltpu.VMEM((tok_rows, width), jnp.bfloat16),
            pltpu.VMEM((1, width), jnp.float32),
            pltpu.VMEM((top_count, tok_rows), jnp.int32),
            pltpu.SemaphoreType.DMA((3,)),
        ],
        compiler_params=pltpu.CompilerParams(vmem_limit_bytes=8 * 1024 * 1024),
        name="route",
    )(*[pltpu.with_memory_space_constraint(x, pltpu.HBM) for x in (hidden_in, norm_gain.reshape(1, width), ids)])
    weights = pl.pallas_call(
        functools.partial(gate_kernel, capacity),
        out_shape=jax.ShapeDtypeStruct((2, 3, 8 * RING * capacity, tok_rows), jnp.bfloat16),
        compiler_params=pltpu.CompilerParams(vmem_limit_bytes=4 * 1024 * 1024),
    name="gates",
    )(normed, router_weight.T, ids)
    gate_local = gate_proj[0]
    up_local = up_proj[0]
    down_local = down_proj[0]
    other = other_core(other)
    both = [jnp.concatenate([same[i], other[i]], axis=0) for i in range(RING)]
    moved = [unpack(along_x(pack(both[i]), step)) for i, step in ((2, 1), (1, -1), (3, 2))]
    arrived = [jnp.concatenate([both[0], moved[0]], axis=0), jnp.concatenate(moved[1:], axis=0)]
    arrived = [lax.optimization_barrier(value) for value in arrived]
    part = rows // 2
    orders = (("z", "y"), ("y", "z"))
    gathered = [gather_ring(arrived[i], *orders[i]) for i in range(2)]
    stages = []
    for stage in range(3):
        value = jnp.concatenate(gathered[0][stage] + gathered[1][stage], axis=0)
        gate = jnp.dot(value, gate_local, preferred_element_type=jnp.float32)
        upper = jnp.dot(value, up_local, preferred_element_type=jnp.float32)
        act = (jax.nn.silu(gate) * upper).astype(jnp.bfloat16)
        stages.append(act.reshape(2, -1, RING, part, act.shape[1]))
    answers = reduce_rings(stages, down_local, orders, part)
    half = part // 2
    back = [
        pack(answers[0][:half]),
        along_x(pack(answers[1][:half]), 1),
        along_x(pack(answers[0][half:]), -1),
        along_x(pack(answers[1][half:]), 2),
    ]
    back[0] = lax.optimization_barrier(back[0])
    crossed = other_core(jnp.concatenate(back, axis=0))
    return pl.pallas_call(
        mix_kernel,
        out_shape=jax.ShapeDtypeStruct((tok_rows, width), jnp.bfloat16),
        scratch_shapes=[pltpu.VMEM((8 * RING * capacity, width // 2), jnp.bfloat16)],
        compiler_params=pltpu.CompilerParams(vmem_limit_bytes=8 * 1024 * 1024),
        name="mix",
    )(hidden_in, weights, *back, crossed)


def solution(mesh):
    placed = (
        P(("expert", "hidden"), None),
        P(),
        P(),
        P(("expert", "hidden"), None),
        P("expert", None, "hidden"),
        P("expert", None, "hidden"),
        P("expert", "hidden", None),
    )

    return jax.shard_map(
        per_device,
        mesh=mesh,
        in_specs=placed,
        out_specs=P(("expert", "hidden"), None),
        check_vma=False,
    )
```

```python
import functools

import jax
import jax.numpy as jnp
from jax import lax
from jax.experimental import pallas as pl
from jax.experimental.pallas import tpu as pltpu
from jax.sharding import PartitionSpec as P


RING = 4


PAD = 8
CHUNK = 512
MIX = 1024


def slots(ids_ref):
    first, second = ids_ref[0:1, :], ids_ref[1:2, :]
    tokens = first.shape[1]
    down = lax.broadcasted_iota(jnp.int32, (tokens, tokens), 0)
    across = lax.broadcasted_iota(jnp.int32, (tokens, tokens), 1)

    def column(row):
        return jnp.sum(jnp.where(down == across, row, 0), axis=1, keepdims=True)

    first_col, second_col = column(first), column(second)
    here = lax.axis_index("expert")
    found = []
    for ids, extra in ((first, 0), (second, (first == second).astype(jnp.int32))):
        same = (first_col == ids).astype(jnp.int32) + (second_col == ids).astype(jnp.int32)
        rank = jnp.sum(jnp.where(down < across, same, 0), axis=0, keepdims=True) + extra
        offset = ((ids >> 1) - (here >> 1)) & (RING - 1)
        place = jnp.where(offset == 0, 0, jnp.where(offset == RING - 1, 1, offset + 1))
        found.append((place, (ids & 1) ^ (here & 1), rank))
    return found


def route_kernel(
    hidden_hbm, gain_hbm, ids_hbm, same_ref, other_ref, normed_ref, hidden_ref, gain_ref, ids_ref, sems
):
    pairs = ((hidden_hbm, hidden_ref), (gain_hbm, gain_ref), (ids_hbm, ids_ref))
    copies = [pltpu.make_async_copy(source, target, sems.at[i]) for i, (source, target) in enumerate(pairs)]
    for copy in copies:
        copy.start()
    for copy in copies:
        copy.wait()
    count, capacity, width = same_ref.shape
    tokens = hidden_ref.shape[0]
    values = hidden_ref[...].astype(jnp.float32)
    factor = lax.rsqrt(jnp.sum(values * values, axis=1, keepdims=True) / width + 1e-05)
    normed_ref[...] = (values * factor * gain_ref[...]).astype(jnp.bfloat16)
    first, second = [(core * count + place) * PAD + rank for place, core, rank in slots(ids_ref)]
    row = lax.broadcasted_iota(jnp.int32, (2 * count * PAD, tokens), 0)
    pick = jnp.where((row == first) | (row == second), 1.0, 0.0).astype(jnp.bfloat16)

    @pl.loop(0, width // CHUNK)
    def _(step):
        columns = pl.ds(pl.multiple_of(step * CHUNK, CHUNK), CHUNK)
        rows = jnp.dot(pick, normed_ref[:, columns], preferred_element_type=jnp.float32)
        for i in range(count):
            for core, out_ref in ((0, same_ref), (1, other_ref)):
                start = (core * count + i) * PAD
                out_ref[i, :, columns] = rows[start : start + capacity].astype(jnp.bfloat16)


def gate_kernel(capacity, normed_ref, router_ref, ids_ref, out_ref):
    logits = lax.dot_general(
        router_ref[...], normed_ref[...], (((1,), (1,)), ((), ())), preferred_element_type=jnp.float32
    )
    expert = lax.broadcasted_iota(jnp.int32, logits.shape, 0)
    chosen = [
        jnp.sum(jnp.where(expert == ids_ref[k : k + 1, :], logits, 0.0), axis=0, keepdims=True)
        for k in range(2)
    ]
    gate = 1.0 / (1.0 + jnp.exp(chosen[1] - chosen[0]))
    found = slots(ids_ref)
    row = lax.broadcasted_iota(jnp.int32, out_ref.shape[2:], 0)
    for half in range(2):
        first, second = [
            (core * RING + place) * 4 * capacity + (2 * half + core) * capacity + rank
            for place, core, rank in found
        ]
        rest = jnp.where(row == first, gate, 0.0) + jnp.where(row == second, 1.0 - gate, 0.0)
        for term in range(3):
            part = rest.astype(jnp.bfloat16)
            out_ref[half, term] = part
            rest = rest - part.astype(jnp.float32)


def mix_kernel(hidden_ref, weight_ref, own_ref, below_ref, above_ref, across_ref, other_ref, out_ref, held_ref):
    half = held_ref.shape[1]
    start = 0
    for ref in (own_ref, below_ref, above_ref, across_ref, other_ref):
        held_ref[start : start + ref.shape[0], :] = ref[...]
        start += ref.shape[0]

    @pl.loop(0, half // MIX)
    def _(step):
        rows = held_ref[:, pl.ds(pl.multiple_of(step * MIX, MIX), MIX)]
        for side in range(2):
            columns = pl.ds(pl.multiple_of(side * half + step * MIX, MIX), MIX)
            total = hidden_ref[:, columns].astype(jnp.float32)
            mixed = 0.0
            for term in (2, 1, 0):
                mixed = mixed + lax.dot_general(
                    weight_ref[side, term],
                    rows,
                    (((0,), (0,)), ((), ())),
                    preferred_element_type=jnp.float32,
                )
            out_ref[:, columns] = (total + mixed).astype(jnp.bfloat16)


def along_x(value, step):
    pairs = [(2 * x + c, 2 * ((x + step) % RING) + c) for x in range(RING) for c in range(2)]
    return lax.ppermute(value, "expert", pairs)


def other_core(value):
    return lax.ppermute(value, "expert", [(i, i ^ 1) for i in range(2 * RING)])


def shift(value, axis, step):
    def target(i):
        z, y = divmod(i, RING)
        return ((z + step) % RING) * RING + y if axis == "z" else z * RING + (y + step) % RING

    return lax.ppermute(value, "hidden", [(i, target(i)) for i in range(RING * RING)])


def gather_ring(own, first, second):
    below, above = shift(own, first, 1), shift(own, first, -1)
    far = shift(own, first, 2)
    near = lax.optimization_barrier(jnp.concatenate([own, below, above], axis=0))
    rows = own.shape[0]
    below, above = [shift(near, second, 1)], [shift(near, second, -1)]
    below.append(shift(far, second, 1))
    above.append(shift(far, second, -1))
    last = [
        shift(below[0][: 2 * rows], second, 1),
        shift(jnp.concatenate([above[0][2 * rows :], above[1]], axis=0), second, -1),
    ]
    return [near, far], below + above, last


def add(*terms):
    total = terms[0].astype(jnp.float32)
    for term in terms[1:]:
        total = total + term.astype(jnp.float32)
    return total.astype(jnp.bfloat16)


def reduce_rings(stages, down, orders, rows):
    start, middle, end = stages
    both = range(2)

    def product(blocks):
        value = [block.reshape(-1, block.shape[-1]) for block in blocks]
        value = jnp.dot(jnp.concatenate(value, axis=0), down, preferred_element_type=jnp.float32)
        return lax.optimization_barrier(value.astype(jnp.bfloat16))

    def piece(value, base, count):
        return value[base * rows : (base + count) * rows]

    early = product([middle[:, :, 1:].swapaxes(1, 2), start[:, 0, 2:]])
    up_one = [shift(piece(early, 6 * i + 4, 2), orders[i][0], 1) for i in both]
    down_one = [
        shift(jnp.concatenate([piece(early, 13 + 2 * i, 1), piece(early, 6 * i, 2)], axis=0), orders[i][0], -1)
        for i in both
    ]
    up_own = [shift(piece(early, 12 + 2 * i, 1), orders[i][0], 1) for i in both]
    late = product([end[:, 0, 1:], start[:, 0, 1]])
    down_two = [shift(piece(late, 3 * i + 2, 1), orders[i][0], -1) for i in both]
    up_sum = [add(piece(early, 6 * i + 2, 2), up_one[i]) for i in both]
    up_three = [shift(up_sum[i], orders[i][0], 1) for i in both]
    up_two = [shift(piece(late, 3 * i + 1, 1), orders[i][0], 1) for i in both]
    soon = [lax.optimization_barrier(piece(late, 6 + i, 1)) for i in both]
    down_own = [shift(add(soon[i], down_one[i][:rows]), orders[i][0], -1) for i in both]
    down_sum = [add(piece(late, 3 * i, 1), down_two[i]) for i in both]
    down_far = [shift(down_sum[i], orders[i][0], -1) for i in both]
    kept = [product([start[i, 0, 0], end[i, 0, 0], middle[i, :, 0]]) for i in both]
    sides = []
    for i in both:
        inner = add(kept[i][2 * rows :], up_three[i], down_one[i][rows:])
        sides.append((shift(inner[rows:], orders[i][1], 1), shift(inner[:rows], orders[i][1], -1)))
    results = []
    for i in both:
        across = add(kept[i][rows : 2 * rows], up_two[i], down_far[i])
        across = shift(across, orders[i][1], 2)
        own = lax.optimization_barrier(add(kept[i][:rows], up_own[i], down_own[i]))
        results.append(add(own, *sides[i], across))
    return results


def pack(value):
    half = value.shape[1] // 2
    return jnp.concatenate([value[:, :half], value[:, half:]], axis=0)


def unpack(value):
    half = value.shape[0] // 2
    return jnp.concatenate([value[:half], value[half:]], axis=1)


def per_device(hidden_in, norm_gain, router_weight, expert_ids, gate_proj, up_proj, down_proj):
    experts = lax.axis_size("expert")
    tok_rows = hidden_in.shape[0]
    width = hidden_in.shape[1]
    top_count = expert_ids.shape[1]
    capacity = 3 * tok_rows * top_count // (2 * experts)
    rows = experts * capacity
    ids = expert_ids.T
    piece = jax.ShapeDtypeStruct((RING, capacity, width), jnp.bfloat16)
    same, other, normed = pl.pallas_call(
        route_kernel,
        out_shape=(piece, piece, jax.ShapeDtypeStruct((tok_rows, width), jnp.bfloat16)),
        in_specs=[pl.BlockSpec(memory_space=pltpu.HBM)] * 3,
        scratch_shapes=[
            pltpu.VMEM((tok_rows, width), jnp.bfloat16),
            pltpu.VMEM((1, width), jnp.float32),
            pltpu.VMEM((top_count, tok_rows), jnp.int32),
            pltpu.SemaphoreType.DMA((3,)),
        ],
        compiler_params=pltpu.CompilerParams(vmem_limit_bytes=8 * 1024 * 1024),
        name="route",
    )(*[pltpu.with_memory_space_constraint(x, pltpu.HBM) for x in (hidden_in, norm_gain.reshape(1, width), ids)])
    weights = pl.pallas_call(
        functools.partial(gate_kernel, capacity),
        out_shape=jax.ShapeDtypeStruct((2, 3, 8 * RING * capacity, tok_rows), jnp.bfloat16),
        compiler_params=pltpu.CompilerParams(vmem_limit_bytes=4 * 1024 * 1024),
    name="gates",
    )(normed, router_weight.T, ids)
    gate_local = gate_proj[0]
    up_local = up_proj[0]
    down_local = down_proj[0]
    other = other_core(other)
    both = [jnp.concatenate([same[i], other[i]], axis=0) for i in range(RING)]
    moved = [unpack(along_x(pack(both[i]), step)) for i, step in ((2, 1), (1, -1), (3, 2))]
    arrived = [jnp.concatenate([both[0], moved[0]], axis=0), jnp.concatenate(moved[1:], axis=0)]
    arrived = [lax.optimization_barrier(value) for value in arrived]
    part = rows // 2
    orders = (("z", "y"), ("y", "z"))
    gathered = [gather_ring(arrived[i], *orders[i]) for i in range(2)]
    stages = []
    for stage in range(3):
        value = jnp.concatenate(gathered[0][stage] + gathered[1][stage], axis=0)
        gate = jnp.dot(value, gate_local, preferred_element_type=jnp.float32)
        upper = jnp.dot(value, up_local, preferred_element_type=jnp.float32)
        act = (jax.nn.silu(gate) * upper).astype(jnp.bfloat16)
        stages.append(act.reshape(2, -1, RING, part, act.shape[1]))
    answers = reduce_rings(stages, down_local, orders, part)
    half = part // 2
    back = [
        pack(answers[0][:half]),
        along_x(pack(answers[1][:half]), 1),
        along_x(pack(answers[0][half:]), -1),
        along_x(pack(answers[1][half:]), 2),
    ]
    back[0] = lax.optimization_barrier(back[0])
    crossed = other_core(jnp.concatenate(back, axis=0))
    return pl.pallas_call(
        mix_kernel,
        out_shape=jax.ShapeDtypeStruct((tok_rows, width), jnp.bfloat16),
        scratch_shapes=[pltpu.VMEM((8 * RING * capacity, width // 2), jnp.bfloat16)],
        compiler_params=pltpu.CompilerParams(vmem_limit_bytes=8 * 1024 * 1024),
        name="mix",
    )(hidden_in, weights, *back, crossed)


def solution(mesh):
    placed = (
        P(("expert", "hidden"), None),
        P(),
        P(),
        P(("expert", "hidden"), None),
        P("expert", None, "hidden"),
        P("expert", None, "hidden"),
        P("expert", "hidden", None),
    )

    return jax.shard_map(
        per_device,
        mesh=mesh,
        in_specs=placed,
        out_specs=P(("expert", "hidden"), None),
        check_vma=False,
    )
```

```python
import functools

import jax
import jax.numpy as jnp
from jax import lax
from jax.experimental import pallas as pl
from jax.experimental.pallas import tpu as pltpu
from jax.sharding import PartitionSpec as P


RING = 4


PAD = 8
CHUNK = 1536
MIX = 1024


def slots(ids_ref):
    first, second = ids_ref[0:1, :], ids_ref[1:2, :]
    tokens = first.shape[1]
    down = lax.broadcasted_iota(jnp.int32, (tokens, tokens), 0)
    across = lax.broadcasted_iota(jnp.int32, (tokens, tokens), 1)

    def column(row):
        return jnp.sum(jnp.where(down == across, row, 0), axis=1, keepdims=True)

    first_col, second_col = column(first), column(second)
    here = lax.axis_index("expert")
    found = []
    for ids, extra in ((first, 0), (second, (first == second).astype(jnp.int32))):
        same = (first_col == ids).astype(jnp.int32) + (second_col == ids).astype(jnp.int32)
        rank = jnp.sum(jnp.where(down < across, same, 0), axis=0, keepdims=True) + extra
        offset = ((ids >> 1) - (here >> 1)) & (RING - 1)
        place = jnp.where(offset == 0, 0, jnp.where(offset == RING - 1, 1, offset + 1))
        found.append((place, (ids & 1) ^ (here & 1), rank))
    return found


def route_kernel(
    hidden_hbm, gain_hbm, ids_hbm, same_ref, other_ref, normed_ref, hidden_ref, gain_ref, ids_ref, sems
):
    pairs = ((hidden_hbm, hidden_ref), (gain_hbm, gain_ref), (ids_hbm, ids_ref))
    copies = [pltpu.make_async_copy(source, target, sems.at[i]) for i, (source, target) in enumerate(pairs)]
    for copy in copies:
        copy.start()
    for copy in copies:
        copy.wait()
    count, capacity, width = same_ref.shape
    tokens = hidden_ref.shape[0]
    values = hidden_ref[...].astype(jnp.float32)
    factor = lax.rsqrt(jnp.sum(values * values, axis=1, keepdims=True) / width + 1e-05)
    normed_ref[...] = (values * factor * gain_ref[...]).astype(jnp.bfloat16)
    first, second = [(core * count + place) * PAD + rank for place, core, rank in slots(ids_ref)]
    row = lax.broadcasted_iota(jnp.int32, (2 * count * PAD, tokens), 0)
    pick = jnp.where((row == first) | (row == second), 1.0, 0.0).astype(jnp.bfloat16)

    @pl.loop(0, width // CHUNK)
    def _(step):
        columns = pl.ds(pl.multiple_of(step * CHUNK, CHUNK), CHUNK)
        rows = jnp.dot(pick, normed_ref[:, columns], preferred_element_type=jnp.float32)
        for i in range(count):
            for core, out_ref in ((0, same_ref), (1, other_ref)):
                start = (core * count + i) * PAD
                out_ref[i, :, columns] = rows[start : start + capacity].astype(jnp.bfloat16)


def gate_kernel(capacity, normed_ref, router_ref, ids_ref, out_ref):
    logits = lax.dot_general(
        router_ref[...], normed_ref[...], (((1,), (1,)), ((), ())), preferred_element_type=jnp.float32
    )
    expert = lax.broadcasted_iota(jnp.int32, logits.shape, 0)
    chosen = [
        jnp.sum(jnp.where(expert == ids_ref[k : k + 1, :], logits, 0.0), axis=0, keepdims=True)
        for k in range(2)
    ]
    gate = 1.0 / (1.0 + jnp.exp(chosen[1] - chosen[0]))
    found = slots(ids_ref)
    row = lax.broadcasted_iota(jnp.int32, out_ref.shape[2:], 0)
    for half in range(2):
        first, second = [
            (core * RING + place) * 4 * capacity + (2 * half + core) * capacity + rank
            for place, core, rank in found
        ]
        rest = jnp.where(row == first, gate, 0.0) + jnp.where(row == second, 1.0 - gate, 0.0)
        for term in range(3):
            part = rest.astype(jnp.bfloat16)
            out_ref[half, term] = part
            rest = rest - part.astype(jnp.float32)


def mix_kernel(hidden_ref, weight_ref, own_ref, below_ref, above_ref, across_ref, other_ref, out_ref, held_ref):
    half = held_ref.shape[1]
    start = 0
    for ref in (own_ref, below_ref, above_ref, across_ref, other_ref):
        held_ref[start : start + ref.shape[0], :] = ref[...]
        start += ref.shape[0]

    tokens = hidden_ref.shape[0]

    @pl.loop(0, half // MIX)
    def _(step):
        rows = held_ref[:, pl.ds(pl.multiple_of(step * MIX, MIX), MIX)]
        terms = lax.dot_general(
            weight_ref[...], rows, (((0,), (0,)), ((), ())), preferred_element_type=jnp.float32
        )
        for side in range(2):
            columns = pl.ds(pl.multiple_of(side * half + step * MIX, MIX), MIX)
            mixed = 0.0
            for term in (2, 1, 0):
                first = (3 * side + term) * tokens
                mixed = mixed + terms[first : first + tokens]
            out_ref[:, columns] = (hidden_ref[:, columns].astype(jnp.float32) + mixed).astype(jnp.bfloat16)


def along_x(value, step):
    pairs = [(2 * x + c, 2 * ((x + step) % RING) + c) for x in range(RING) for c in range(2)]
    return lax.ppermute(value, "expert", pairs)


def other_core(value):
    return lax.ppermute(value, "expert", [(i, i ^ 1) for i in range(2 * RING)])


def shift(value, axis, step):
    def target(i):
        z, y = divmod(i, RING)
        return ((z + step) % RING) * RING + y if axis == "z" else z * RING + (y + step) % RING

    return lax.ppermute(value, "hidden", [(i, target(i)) for i in range(RING * RING)])


def gather_ring(own, first, second):
    half = own.shape[1] // 2
    below, above = shift(own, first, 1), shift(own, first, -1)
    across = [shift(below[:, :half], first, 1), shift(above[:, half:], first, -1)]
    near = lax.optimization_barrier(jnp.concatenate([own, below, above], axis=0))
    far = jnp.concatenate(across, axis=1)
    rows = own.shape[0]
    below, above = [shift(near, second, 1)], [shift(near, second, -1)]
    below.append(shift(far, second, 1))
    above.append(shift(far, second, -1))
    last = [
        shift(below[0][: 2 * rows], second, 1),
        shift(jnp.concatenate([above[0][2 * rows :], above[1]], axis=0), second, -1),
    ]
    return [near, far], below + above, last


def add(*terms):
    total = terms[0].astype(jnp.float32)
    for term in terms[1:]:
        total = total + term.astype(jnp.float32)
    return total.astype(jnp.bfloat16)


def reduce_rings(stages, down, orders, rows):
    start, middle, end = stages
    both = range(2)

    def product(blocks):
        value = [block.reshape(-1, block.shape[-1]) for block in blocks]
        value = jnp.dot(jnp.concatenate(value, axis=0), down, preferred_element_type=jnp.float32)
        return lax.optimization_barrier(value.astype(jnp.bfloat16))

    def piece(value, base, count):
        return value[base * rows : (base + count) * rows]

    early = product([middle[:, :, 1:].swapaxes(1, 2), start[:, 0, 2:]])
    up_one = [shift(piece(early, 6 * i + 4, 2), orders[i][0], 1) for i in both]
    down_one = [
        shift(jnp.concatenate([piece(early, 13 + 2 * i, 1), piece(early, 6 * i, 2)], axis=0), orders[i][0], -1)
        for i in both
    ]
    up_own = [shift(piece(early, 12 + 2 * i, 1), orders[i][0], 1) for i in both]
    late = product([end[:, 0, 1:], start[:, 0, 1]])
    down_two = [shift(piece(late, 3 * i + 2, 1), orders[i][0], -1) for i in both]
    up_sum = [add(piece(early, 6 * i + 2, 2), up_one[i]) for i in both]
    up_three = [shift(up_sum[i], orders[i][0], 1) for i in both]
    up_two = [shift(piece(late, 3 * i + 1, 1), orders[i][0], 1) for i in both]
    down_sum = [
        jnp.concatenate(
            [add(piece(late, 6 + i, 1), down_one[i][:rows]), add(piece(late, 3 * i, 1), down_two[i])], axis=0
        )
        for i in both
    ]
    down_three = [shift(down_sum[i], orders[i][0], -1) for i in both]
    kept = [product([start[i, 0, 0], end[i, 0, 0], middle[i, :, 0]]) for i in both]
    sides = []
    for i in both:
        inner = add(kept[i][2 * rows :], up_three[i], down_one[i][rows:])
        sides.append((shift(inner[rows:], orders[i][1], 1), shift(inner[:rows], orders[i][1], -1)))
    results = []
    for i in both:
        across = add(kept[i][rows : 2 * rows], up_two[i], down_three[i][rows:])
        across = shift(across, orders[i][1], 2)
        own = lax.optimization_barrier(add(kept[i][:rows], up_own[i], down_three[i][:rows]))
        results.append(add(own, *sides[i], across))
    return results


def pack(value):
    half = value.shape[1] // 2
    return jnp.concatenate([value[:, :half], value[:, half:]], axis=0)


def unpack(value):
    half = value.shape[0] // 2
    return jnp.concatenate([value[:half], value[half:]], axis=1)


def per_device(hidden_in, norm_gain, router_weight, expert_ids, gate_proj, up_proj, down_proj):
    experts = lax.axis_size("expert")
    tok_rows = hidden_in.shape[0]
    width = hidden_in.shape[1]
    top_count = expert_ids.shape[1]
    capacity = 3 * tok_rows * top_count // (2 * experts)
    rows = experts * capacity
    ids = expert_ids.T
    piece = jax.ShapeDtypeStruct((RING, capacity, width), jnp.bfloat16)
    same, other, normed = pl.pallas_call(
        route_kernel,
        out_shape=(piece, piece, jax.ShapeDtypeStruct((tok_rows, width), jnp.bfloat16)),
        in_specs=[pl.BlockSpec(memory_space=pltpu.HBM)] * 3,
        scratch_shapes=[
            pltpu.VMEM((tok_rows, width), jnp.bfloat16),
            pltpu.VMEM((1, width), jnp.float32),
            pltpu.VMEM((top_count, tok_rows), jnp.int32),
            pltpu.SemaphoreType.DMA((3,)),
        ],
        compiler_params=pltpu.CompilerParams(vmem_limit_bytes=8 * 1024 * 1024),
        name="route",
    )(*[pltpu.with_memory_space_constraint(x, pltpu.HBM) for x in (hidden_in, norm_gain.reshape(1, width), ids)])
    weights = pl.pallas_call(
        functools.partial(gate_kernel, capacity),
        out_shape=jax.ShapeDtypeStruct((2, 3, 8 * RING * capacity, tok_rows), jnp.bfloat16),
        compiler_params=pltpu.CompilerParams(vmem_limit_bytes=4 * 1024 * 1024),
    name="gates",
    )(normed, router_weight.T, ids)
    weights = weights.transpose(2, 0, 1, 3).reshape(weights.shape[2], -1)
    gate_local = gate_proj[0]
    up_local = up_proj[0]
    down_local = down_proj[0]
    other = other_core(other)
    both = [jnp.concatenate([same[i], other[i]], axis=0) for i in range(RING)]
    moved = [unpack(along_x(pack(both[i]), step)) for i, step in ((2, 1), (1, -1), (3, 2))]
    arrived = [jnp.concatenate([both[0], moved[0]], axis=0), jnp.concatenate(moved[1:], axis=0)]
    arrived = [lax.optimization_barrier(value) for value in arrived]
    part = rows // 2
    orders = (("z", "y"), ("y", "z"))
    gathered = [gather_ring(arrived[i], *orders[i]) for i in range(2)]
    stages = []
    for stage in range(3):
        value = jnp.concatenate(gathered[0][stage] + gathered[1][stage], axis=0)
        gate = jnp.dot(value, gate_local, preferred_element_type=jnp.float32)
        upper = jnp.dot(value, up_local, preferred_element_type=jnp.float32)
        act = (jax.nn.silu(gate) * upper).astype(jnp.bfloat16)
        stages.append(act.reshape(2, -1, RING, part, act.shape[1]))
    answers = reduce_rings(stages, down_local, orders, part)
    half = part // 2
    back = [
        pack(answers[0][:half]),
        along_x(pack(answers[1][:half]), 1),
        along_x(pack(answers[0][half:]), -1),
        along_x(pack(answers[1][half:]), 2),
    ]
    back[0] = lax.optimization_barrier(back[0])
    crossed = other_core(jnp.concatenate(back, axis=0))
    return pl.pallas_call(
        mix_kernel,
        out_shape=jax.ShapeDtypeStruct((tok_rows, width), jnp.bfloat16),
        scratch_shapes=[pltpu.VMEM((8 * RING * capacity, width // 2), jnp.bfloat16)],
        compiler_params=pltpu.CompilerParams(vmem_limit_bytes=8 * 1024 * 1024),
        name="mix",
    )(hidden_in, weights, *back, crossed)


def solution(mesh):
    placed = (
        P(("expert", "hidden"), None),
        P(),
        P(),
        P(("expert", "hidden"), None),
        P("expert", None, "hidden"),
        P("expert", None, "hidden"),
        P("expert", "hidden", None),
    )

    return jax.shard_map(
        per_device,
        mesh=mesh,
        in_specs=placed,
        out_specs=P(("expert", "hidden"), None),
        check_vma=False,
    )
```

```python
import functools

import jax
import jax.numpy as jnp
from jax import lax
from jax.experimental import pallas as pl
from jax.experimental.pallas import tpu as pltpu
from jax.sharding import PartitionSpec as P


RING = 4


PAD = 8
CHUNK = 1536
MIX = 1024


def slots(ids_ref):
    first, second = ids_ref[0:1, :], ids_ref[1:2, :]
    tokens = first.shape[1]
    down = lax.broadcasted_iota(jnp.int32, (tokens, tokens), 0)
    across = lax.broadcasted_iota(jnp.int32, (tokens, tokens), 1)

    def column(row):
        return jnp.sum(jnp.where(down == across, row, 0), axis=1, keepdims=True)

    first_col, second_col = column(first), column(second)
    here = lax.axis_index("expert")
    found = []
    for ids, extra in ((first, 0), (second, (first == second).astype(jnp.int32))):
        same = (first_col == ids).astype(jnp.int32) + (second_col == ids).astype(jnp.int32)
        rank = jnp.sum(jnp.where(down < across, same, 0), axis=0, keepdims=True) + extra
        offset = ((ids >> 1) - (here >> 1)) & (RING - 1)
        place = jnp.where(offset == 0, 0, jnp.where(offset == RING - 1, 1, offset + 1))
        found.append((place, (ids & 1) ^ (here & 1), rank))
    return found


def route_kernel(
    hidden_hbm, gain_hbm, ids_hbm, same_ref, other_ref, normed_ref, hidden_ref, gain_ref, ids_ref, sems
):
    pairs = ((hidden_hbm, hidden_ref), (gain_hbm, gain_ref), (ids_hbm, ids_ref))
    copies = [pltpu.make_async_copy(source, target, sems.at[i]) for i, (source, target) in enumerate(pairs)]
    for copy in copies:
        copy.start()
    for copy in copies:
        copy.wait()
    count, capacity, width = same_ref.shape
    tokens = hidden_ref.shape[0]
    values = hidden_ref[...].astype(jnp.float32)
    factor = lax.rsqrt(jnp.sum(values * values, axis=1, keepdims=True) / width + 1e-05)
    normed_ref[...] = (values * factor * gain_ref[...]).astype(jnp.bfloat16)
    first, second = [(core * count + place) * PAD + rank for place, core, rank in slots(ids_ref)]
    row = lax.broadcasted_iota(jnp.int32, (2 * count * PAD, tokens), 0)
    pick = jnp.where((row == first) | (row == second), 1.0, 0.0).astype(jnp.bfloat16)

    @pl.loop(0, width // CHUNK)
    def _(step):
        columns = pl.ds(pl.multiple_of(step * CHUNK, CHUNK), CHUNK)
        rows = jnp.dot(pick, normed_ref[:, columns], preferred_element_type=jnp.float32)
        for i in range(count):
            for core, out_ref in ((0, same_ref), (1, other_ref)):
                start = (core * count + i) * PAD
                out_ref[i, :, columns] = rows[start : start + capacity].astype(jnp.bfloat16)


def gate_kernel(capacity, normed_ref, router_ref, ids_ref, out_ref):
    logits = lax.dot_general(
        router_ref[...], normed_ref[...], (((1,), (1,)), ((), ())), preferred_element_type=jnp.float32
    )
    expert = lax.broadcasted_iota(jnp.int32, logits.shape, 0)
    chosen = [
        jnp.sum(jnp.where(expert == ids_ref[k : k + 1, :], logits, 0.0), axis=0, keepdims=True)
        for k in range(2)
    ]
    gate = 1.0 / (1.0 + jnp.exp(chosen[1] - chosen[0]))
    found = slots(ids_ref)
    row = lax.broadcasted_iota(jnp.int32, out_ref.shape[2:], 0)
    for half in range(2):
        first, second = [
            (core * RING + place) * 4 * capacity + (2 * half + core) * capacity + rank
            for place, core, rank in found
        ]
        rest = jnp.where(row == first, gate, 0.0) + jnp.where(row == second, 1.0 - gate, 0.0)
        for term in range(3):
            part = rest.astype(jnp.bfloat16)
            out_ref[half, term] = part
            rest = rest - part.astype(jnp.float32)


def mix_kernel(hidden_ref, weight_ref, own_ref, below_ref, above_ref, across_ref, other_ref, out_ref, held_ref):
    half = held_ref.shape[1]
    start = 0
    for ref in (own_ref, below_ref, above_ref, across_ref, other_ref):
        held_ref[start : start + ref.shape[0], :] = ref[...]
        start += ref.shape[0]

    tokens = hidden_ref.shape[0]

    @pl.loop(0, half // MIX)
    def _(step):
        rows = held_ref[:, pl.ds(pl.multiple_of(step * MIX, MIX), MIX)]
        terms = lax.dot_general(
            weight_ref[...], rows, (((0,), (0,)), ((), ())), preferred_element_type=jnp.float32
        )
        for side in range(2):
            columns = pl.ds(pl.multiple_of(side * half + step * MIX, MIX), MIX)
            mixed = 0.0
            for term in (2, 1, 0):
                first = (3 * side + term) * tokens
                mixed = mixed + terms[first : first + tokens]
            out_ref[:, columns] = (hidden_ref[:, columns].astype(jnp.float32) + mixed).astype(jnp.bfloat16)


def along_x(value, step):
    pairs = [(2 * x + c, 2 * ((x + step) % RING) + c) for x in range(RING) for c in range(2)]
    return lax.ppermute(value, "expert", pairs)


def other_core(value):
    return lax.ppermute(value, "expert", [(i, i ^ 1) for i in range(2 * RING)])


def shift(value, axis, step):
    def target(i):
        z, y = divmod(i, RING)
        return ((z + step) % RING) * RING + y if axis == "z" else z * RING + (y + step) % RING

    return lax.ppermute(value, "hidden", [(i, target(i)) for i in range(RING * RING)])


def gather_ring(own, first, second):
    half = own.shape[1] // 2
    below, above = shift(own, first, 1), shift(own, first, -1)
    across = [shift(below[:, :half], first, 1), shift(above[:, half:], first, -1)]
    near = lax.optimization_barrier(jnp.concatenate([own, below, above], axis=0))
    far = jnp.concatenate(across, axis=1)
    rows = own.shape[0]
    below, above = [shift(near, second, 1)], [shift(near, second, -1)]
    below.append(shift(far, second, 1))
    above.append(shift(far, second, -1))
    last = [shift(below[0][: 2 * rows], second, 1)]
    last.append(shift(jnp.concatenate([above[0][2 * rows :], above[1]], axis=0), second, -1))
    return [near, far], below + above, last


def add(*terms):
    total = terms[0].astype(jnp.float32)
    for term in terms[1:]:
        total = total + term.astype(jnp.float32)
    return total.astype(jnp.bfloat16)


def reduce_rings(stages, down, orders, rows):
    start, middle, end = stages
    both = range(2)

    def product(blocks):
        value = [block.reshape(-1, block.shape[-1]) for block in blocks]
        value = jnp.dot(jnp.concatenate(value, axis=0), down, preferred_element_type=jnp.float32)
        return lax.optimization_barrier(value.astype(jnp.bfloat16))

    def piece(value, base, count):
        return value[base * rows : (base + count) * rows]

    early = product([middle[:, :, 1:].swapaxes(1, 2), start[:, 0, 2:]])
    up_one = [shift(piece(early, 6 * i + 4, 2), orders[i][0], 1) for i in both]
    down_one = [
        shift(jnp.concatenate([piece(early, 13 + 2 * i, 1), piece(early, 6 * i, 2)], axis=0), orders[i][0], -1)
        for i in both
    ]
    up_own = [shift(piece(early, 12 + 2 * i, 1), orders[i][0], 1) for i in both]
    late = product([end[:, 0, 1:], start[:, 0, 1]])
    down_two = [shift(piece(late, 3 * i + 2, 1), orders[i][0], -1) for i in both]
    up_sum = [add(piece(early, 6 * i + 2, 2), up_one[i]) for i in both]
    up_three = [shift(up_sum[i], orders[i][0], 1) for i in both]
    up_two = [shift(piece(late, 3 * i + 1, 1), orders[i][0], 1) for i in both]
    down_sum = [
        jnp.concatenate(
            [add(piece(late, 6 + i, 1), down_one[i][:rows]), add(piece(late, 3 * i, 1), down_two[i])], axis=0
        )
        for i in both
    ]
    down_three = [shift(down_sum[i], orders[i][0], -1) for i in both]
    kept = [product([start[i, 0, 0], end[i, 0, 0], middle[i, :, 0]]) for i in both]
    sides = []
    for i in both:
        inner = add(kept[i][2 * rows :], up_three[i], down_one[i][rows:])
        sides.append((shift(inner[rows:], orders[i][1], 1), shift(inner[:rows], orders[i][1], -1)))
    results = []
    for i in both:
        across = add(kept[i][rows : 2 * rows], up_two[i], down_three[i][rows:])
        across = shift(across, orders[i][1], 2)
        own = lax.optimization_barrier(add(kept[i][:rows], up_own[i], down_three[i][:rows]))
        results.append(add(own, *sides[i], across))
    return results


def pack(value):
    half = value.shape[1] // 2
    return jnp.concatenate([value[:, :half], value[:, half:]], axis=0)


def unpack(value):
    half = value.shape[0] // 2
    return jnp.concatenate([value[:half], value[half:]], axis=1)


def per_device(hidden_in, norm_gain, router_weight, expert_ids, gate_proj, up_proj, down_proj):
    experts = lax.axis_size("expert")
    tok_rows = hidden_in.shape[0]
    width = hidden_in.shape[1]
    top_count = expert_ids.shape[1]
    capacity = 3 * tok_rows * top_count // (2 * experts)
    rows = experts * capacity
    ids = expert_ids.T
    piece = jax.ShapeDtypeStruct((RING, capacity, width), jnp.bfloat16)
    same, other, normed = pl.pallas_call(
        route_kernel,
        out_shape=(piece, piece, jax.ShapeDtypeStruct((tok_rows, width), jnp.bfloat16)),
        in_specs=[pl.BlockSpec(memory_space=pltpu.HBM)] * 3,
        scratch_shapes=[
            pltpu.VMEM((tok_rows, width), jnp.bfloat16),
            pltpu.VMEM((1, width), jnp.float32),
            pltpu.VMEM((top_count, tok_rows), jnp.int32),
            pltpu.SemaphoreType.DMA((3,)),
        ],
        compiler_params=pltpu.CompilerParams(vmem_limit_bytes=8 * 1024 * 1024),
        name="route",
    )(*[pltpu.with_memory_space_constraint(x, pltpu.HBM) for x in (hidden_in, norm_gain.reshape(1, width), ids)])
    weights = pl.pallas_call(
        functools.partial(gate_kernel, capacity),
        out_shape=jax.ShapeDtypeStruct((2, 3, 8 * RING * capacity, tok_rows), jnp.bfloat16),
        compiler_params=pltpu.CompilerParams(vmem_limit_bytes=4 * 1024 * 1024),
    name="gates",
    )(normed, router_weight.T, ids)
    weights = weights.transpose(2, 0, 1, 3).reshape(weights.shape[2], -1)
    gate_local = gate_proj[0]
    up_local = up_proj[0]
    down_local = down_proj[0]
    other = other_core(other)
    both = [jnp.concatenate([same[i], other[i]], axis=0) for i in range(RING)]
    moved = [unpack(along_x(pack(both[i]), step)) for i, step in ((2, 1), (1, -1), (3, 2))]
    arrived = [jnp.concatenate([both[0], moved[0]], axis=0), jnp.concatenate(moved[1:], axis=0)]
    arrived = [lax.optimization_barrier(value) for value in arrived]
    part = rows // 2
    orders = (("z", "y"), ("y", "z"))
    gathered = [gather_ring(arrived[i], *orders[i]) for i in range(2)]
    stages = []
    for stage in range(3):
        value = jnp.concatenate(gathered[0][stage] + gathered[1][stage], axis=0)
        gate = jnp.dot(value, gate_local, preferred_element_type=jnp.float32)
        upper = jnp.dot(value, up_local, preferred_element_type=jnp.float32)
        act = (jax.nn.silu(gate) * upper).astype(jnp.bfloat16)
        stages.append(act.reshape(2, -1, RING, part, act.shape[1]))
    answers = reduce_rings(stages, down_local, orders, part)
    half = part // 2
    back = [
        pack(answers[0][:half]),
        along_x(pack(answers[1][:half]), 1),
        along_x(pack(answers[0][half:]), -1),
        along_x(pack(answers[1][half:]), 2),
    ]
    back[0] = lax.optimization_barrier(back[0])
    crossed = other_core(jnp.concatenate(back, axis=0))
    return pl.pallas_call(
        mix_kernel,
        out_shape=jax.ShapeDtypeStruct((tok_rows, width), jnp.bfloat16),
        scratch_shapes=[pltpu.VMEM((8 * RING * capacity, width // 2), jnp.bfloat16)],
        compiler_params=pltpu.CompilerParams(vmem_limit_bytes=8 * 1024 * 1024),
        name="mix",
    )(hidden_in, weights, *back, crossed)


def solution(mesh):
    placed = (
        P(("expert", "hidden"), None),
        P(),
        P(),
        P(("expert", "hidden"), None),
        P("expert", None, "hidden"),
        P("expert", None, "hidden"),
        P("expert", "hidden", None),
    )

    return jax.shard_map(
        per_device,
        mesh=mesh,
        in_specs=placed,
        out_specs=P(("expert", "hidden"), None),
        check_vma=False,
    )
```

```python
import functools

import jax
import jax.numpy as jnp
from jax import lax
from jax.experimental import pallas as pl
from jax.experimental.pallas import tpu as pltpu
from jax.sharding import PartitionSpec as P


RING = 4


PAD = 8
CHUNK = 1536
MIX = 1024


def slots(ids_ref):
    first, second = ids_ref[0:1, :], ids_ref[1:2, :]
    tokens = first.shape[1]
    down = lax.broadcasted_iota(jnp.int32, (tokens, tokens), 0)
    across = lax.broadcasted_iota(jnp.int32, (tokens, tokens), 1)

    def column(row):
        return jnp.sum(jnp.where(down == across, row, 0), axis=1, keepdims=True)

    first_col, second_col = column(first), column(second)
    here = lax.axis_index("expert")
    found = []
    for ids, extra in ((first, 0), (second, (first == second).astype(jnp.int32))):
        same = (first_col == ids).astype(jnp.int32) + (second_col == ids).astype(jnp.int32)
        rank = jnp.sum(jnp.where(down < across, same, 0), axis=0, keepdims=True) + extra
        offset = ((ids >> 1) - (here >> 1)) & (RING - 1)
        place = jnp.where(offset == 0, 0, jnp.where(offset == RING - 1, 1, offset + 1))
        found.append((place, (ids & 1) ^ (here & 1), rank))
    return found


def route_kernel(
    hidden_hbm, gain_hbm, ids_hbm, same_ref, other_ref, normed_ref, hidden_ref, gain_ref, ids_ref, sems
):
    pairs = ((hidden_hbm, hidden_ref), (gain_hbm, gain_ref), (ids_hbm, ids_ref))
    copies = [pltpu.make_async_copy(source, target, sems.at[i]) for i, (source, target) in enumerate(pairs)]
    for copy in copies:
        copy.start()
    for copy in copies:
        copy.wait()
    count, capacity, width = same_ref.shape
    tokens = hidden_ref.shape[0]
    values = hidden_ref[...].astype(jnp.float32)
    factor = lax.rsqrt(jnp.sum(values * values, axis=1, keepdims=True) / width + 1e-05)
    normed_ref[...] = (values * factor * gain_ref[...]).astype(jnp.bfloat16)
    first, second = [(core * count + place) * PAD + rank for place, core, rank in slots(ids_ref)]
    row = lax.broadcasted_iota(jnp.int32, (2 * count * PAD, tokens), 0)
    pick = jnp.where((row == first) | (row == second), 1.0, 0.0).astype(jnp.bfloat16)

    @pl.loop(0, width // CHUNK)
    def _(step):
        columns = pl.ds(pl.multiple_of(step * CHUNK, CHUNK), CHUNK)
        rows = jnp.dot(pick, normed_ref[:, columns], preferred_element_type=jnp.float32)
        for i in range(count):
            for core, out_ref in ((0, same_ref), (1, other_ref)):
                start = (core * count + i) * PAD
                out_ref[i, :, columns] = rows[start : start + capacity].astype(jnp.bfloat16)


def gate_kernel(capacity, normed_ref, router_ref, ids_ref, out_ref):
    logits = lax.dot_general(
        router_ref[...], normed_ref[...], (((1,), (1,)), ((), ())), preferred_element_type=jnp.float32
    )
    expert = lax.broadcasted_iota(jnp.int32, logits.shape, 0)
    chosen = [
        jnp.sum(jnp.where(expert == ids_ref[k : k + 1, :], logits, 0.0), axis=0, keepdims=True)
        for k in range(2)
    ]
    gate = 1.0 / (1.0 + jnp.exp(chosen[1] - chosen[0]))
    found = slots(ids_ref)
    row = lax.broadcasted_iota(jnp.int32, out_ref.shape[2:], 0)
    for half in range(2):
        first, second = [
            (core * RING + place) * 4 * capacity + (2 * half + core) * capacity + rank
            for place, core, rank in found
        ]
        rest = jnp.where(row == first, gate, 0.0) + jnp.where(row == second, 1.0 - gate, 0.0)
        for term in range(3):
            part = rest.astype(jnp.bfloat16)
            out_ref[half, term] = part
            rest = rest - part.astype(jnp.float32)


def mix_kernel(hidden_ref, weight_ref, own_ref, below_ref, above_ref, across_ref, other_ref, out_ref, held_ref):
    half = held_ref.shape[1]
    start = 0
    for ref in (own_ref, below_ref, above_ref, across_ref, other_ref):
        held_ref[start : start + ref.shape[0], :] = ref[...]
        start += ref.shape[0]

    tokens = hidden_ref.shape[0]

    @pl.loop(0, half // MIX)
    def _(step):
        rows = held_ref[:, pl.ds(pl.multiple_of(step * MIX, MIX), MIX)]
        terms = lax.dot_general(
            weight_ref[...], rows, (((0,), (0,)), ((), ())), preferred_element_type=jnp.float32
        )
        for side in range(2):
            columns = pl.ds(pl.multiple_of(side * half + step * MIX, MIX), MIX)
            mixed = 0.0
            for term in (2, 1, 0):
                first = (3 * side + term) * tokens
                mixed = mixed + terms[first : first + tokens]
            out_ref[:, columns] = (hidden_ref[:, columns].astype(jnp.float32) + mixed).astype(jnp.bfloat16)


def along_x(value, step):
    pairs = [(2 * x + c, 2 * ((x + step) % RING) + c) for x in range(RING) for c in range(2)]
    return lax.ppermute(value, "expert", pairs)


def other_core(value):
    return lax.ppermute(value, "expert", [(i, i ^ 1) for i in range(2 * RING)])


def shift(value, axis, step):
    def target(i):
        z, y = divmod(i, RING)
        return ((z + step) % RING) * RING + y if axis == "z" else z * RING + (y + step) % RING

    return lax.ppermute(value, "hidden", [(i, target(i)) for i in range(RING * RING)])


def gather_ring(own, first, second):
    half = own.shape[1] // 2
    below, above = shift(own, first, 1), shift(own, first, -1)
    across = [shift(below[:, :half], first, 1), shift(above[:, half:], first, -1)]
    near = lax.optimization_barrier(jnp.concatenate([own, below, above], axis=0))
    far = jnp.concatenate(across, axis=1)
    rows = own.shape[0]
    below, above = [shift(near, second, 1)], [shift(near, second, -1)]
    below.append(shift(far, second, 1))
    above.append(shift(far, second, -1))
    last = [shift(below[0][: 2 * rows], second, 1)]
    last.append(shift(jnp.concatenate([above[0][2 * rows :], above[1]], axis=0), second, -1))
    return [near, far], below + above, last


def add(*terms):
    total = terms[0].astype(jnp.float32)
    for term in terms[1:]:
        total = total + term.astype(jnp.float32)
    return total.astype(jnp.bfloat16)


def reduce_rings(stages, down, orders, rows):
    start, middle, end = stages
    both = range(2)

    def product(blocks):
        value = [block.reshape(-1, block.shape[-1]) for block in blocks]
        value = jnp.dot(jnp.concatenate(value, axis=0), down, preferred_element_type=jnp.float32)
        return lax.optimization_barrier(value.astype(jnp.bfloat16))

    def piece(value, base, count):
        return value[base * rows : (base + count) * rows]

    early = product([middle[:, :, 1:].swapaxes(1, 2), start[:, 0, 2:]])
    up_one = [shift(piece(early, 6 * i + 4, 2), orders[i][0], 1) for i in both]
    down_one = [
        shift(jnp.concatenate([piece(early, 13 + 2 * i, 1), piece(early, 6 * i, 2)], axis=0), orders[i][0], -1)
        for i in both
    ]
    up_own = [shift(piece(early, 12 + 2 * i, 1), orders[i][0], 1) for i in both]
    late = product([end[:, 0, 1:], start[:, 0, 1]])
    down_two = [shift(piece(late, 3 * i + 2, 1), orders[i][0], -1) for i in both]
    up_sum = [add(piece(early, 6 * i + 2, 2), up_one[i]) for i in both]
    up_three = [shift(up_sum[i], orders[i][0], 1) for i in both]
    up_two = [shift(piece(late, 3 * i + 1, 1), orders[i][0], 1) for i in both]
    soon = [lax.optimization_barrier(piece(late, 6 + i, 1)) for i in both]
    down_own = [shift(add(soon[i], down_one[i][:rows]), orders[i][0], -1) for i in both]
    down_sum = [add(piece(late, 3 * i, 1), down_two[i]) for i in both]
    down_far = [shift(down_sum[i], orders[i][0], -1) for i in both]
    kept = [product([start[i, 0, 0], end[i, 0, 0], middle[i, :, 0]]) for i in both]
    sides = []
    for i in both:
        inner = add(kept[i][2 * rows :], up_three[i], down_one[i][rows:])
        sides.append((shift(inner[rows:], orders[i][1], 1), shift(inner[:rows], orders[i][1], -1)))
    results = []
    for i in both:
        across = add(kept[i][rows : 2 * rows], up_two[i], down_far[i])
        across = shift(across, orders[i][1], 2)
        own = lax.optimization_barrier(add(kept[i][:rows], up_own[i], down_own[i]))
        results.append(add(own, *sides[i], across))
    return results


def pack(value):
    half = value.shape[1] // 2
    return jnp.concatenate([value[:, :half], value[:, half:]], axis=0)


def unpack(value):
    half = value.shape[0] // 2
    return jnp.concatenate([value[:half], value[half:]], axis=1)


def per_device(hidden_in, norm_gain, router_weight, expert_ids, gate_proj, up_proj, down_proj):
    experts = lax.axis_size("expert")
    tok_rows = hidden_in.shape[0]
    width = hidden_in.shape[1]
    top_count = expert_ids.shape[1]
    capacity = 3 * tok_rows * top_count // (2 * experts)
    rows = experts * capacity
    ids = expert_ids.T
    piece = jax.ShapeDtypeStruct((RING, capacity, width), jnp.bfloat16)
    same, other, normed = pl.pallas_call(
        route_kernel,
        out_shape=(piece, piece, jax.ShapeDtypeStruct((tok_rows, width), jnp.bfloat16)),
        in_specs=[pl.BlockSpec(memory_space=pltpu.HBM)] * 3,
        scratch_shapes=[
            pltpu.VMEM((tok_rows, width), jnp.bfloat16),
            pltpu.VMEM((1, width), jnp.float32),
            pltpu.VMEM((top_count, tok_rows), jnp.int32),
            pltpu.SemaphoreType.DMA((3,)),
        ],
        compiler_params=pltpu.CompilerParams(vmem_limit_bytes=8 * 1024 * 1024),
        name="route",
    )(*[pltpu.with_memory_space_constraint(x, pltpu.HBM) for x in (hidden_in, norm_gain.reshape(1, width), ids)])
    weights = pl.pallas_call(
        functools.partial(gate_kernel, capacity),
        out_shape=jax.ShapeDtypeStruct((2, 3, 8 * RING * capacity, tok_rows), jnp.bfloat16),
        compiler_params=pltpu.CompilerParams(vmem_limit_bytes=4 * 1024 * 1024),
    name="gates",
    )(normed, router_weight.T, ids)
    weights = weights.transpose(2, 0, 1, 3).reshape(weights.shape[2], -1)
    gate_local = gate_proj[0]
    up_local = up_proj[0]
    down_local = down_proj[0]
    other = other_core(other)
    both = [jnp.concatenate([same[i], other[i]], axis=0) for i in range(RING)]
    moved = [unpack(along_x(pack(both[i]), step)) for i, step in ((2, 1), (1, -1), (3, 2))]
    arrived = [jnp.concatenate([both[0], moved[0]], axis=0), jnp.concatenate(moved[1:], axis=0)]
    arrived = [lax.optimization_barrier(value) for value in arrived]
    part = rows // 2
    orders = (("z", "y"), ("y", "z"))
    gathered = [gather_ring(arrived[i], *orders[i]) for i in range(2)]
    stages = []
    for stage in range(3):
        value = jnp.concatenate(gathered[0][stage] + gathered[1][stage], axis=0)
        gate = jnp.dot(value, gate_local, preferred_element_type=jnp.float32)
        upper = jnp.dot(value, up_local, preferred_element_type=jnp.float32)
        act = (jax.nn.silu(gate) * upper).astype(jnp.bfloat16)
        stages.append(act.reshape(2, -1, RING, part, act.shape[1]))
    answers = reduce_rings(stages, down_local, orders, part)
    half = part // 2
    back = [
        pack(answers[0][:half]),
        along_x(pack(answers[1][:half]), 1),
        along_x(pack(answers[0][half:]), -1),
        along_x(pack(answers[1][half:]), 2),
    ]
    back[0] = lax.optimization_barrier(back[0])
    crossed = other_core(jnp.concatenate(back, axis=0))
    return pl.pallas_call(
        mix_kernel,
        out_shape=jax.ShapeDtypeStruct((tok_rows, width), jnp.bfloat16),
        scratch_shapes=[pltpu.VMEM((8 * RING * capacity, width // 2), jnp.bfloat16)],
        compiler_params=pltpu.CompilerParams(vmem_limit_bytes=8 * 1024 * 1024),
        name="mix",
    )(hidden_in, weights, *back, crossed)


def solution(mesh):
    placed = (
        P(("expert", "hidden"), None),
        P(),
        P(),
        P(("expert", "hidden"), None),
        P("expert", None, "hidden"),
        P("expert", None, "hidden"),
        P("expert", "hidden", None),
    )

    return jax.shard_map(
        per_device,
        mesh=mesh,
        in_specs=placed,
        out_specs=P(("expert", "hidden"), None),
        check_vma=False,
    )
```
